256 devices in a mesh: gx: 2 (over z_hi), gy: 64 (over z_lo, y, x), vert: 2 (over core).
Axes of the slice: x: 4, y: 4, z: 8 (z_hi: 2, z_lo: 4; z = z_hi * 4 + z_lo), core: 2. Of those that a mesh axis runs over, the one named last changes fastest.
Arguments:
- distribution: float32 [32, 1024, 4096], P('gx', 'gy', 'vert'), may hold values from -6 to 6
- density: float32 [32, 1024], P('gx', 'gy'), may hold values from 0.3 to 3
- cell_type: int32 [32, 1024], P('gx', 'gy'), may hold values from 0 to 2, as said below
- inflow: float32 [4096], P('vert'), may hold values from -6 to 6
Outputs:
- evolved: float32 [32, 1024, 4096], P('gx', 'gy', 'vert')
The draws below stay inside these ranges and needn't reach their ends.
Inputs may be any that keep to these rules, and one draw needn't show every extreme that they name: `cell_type`: 0 marks a gas cell, 1 a wall cell, 2 an inflow cell; most cells are gas cells.
All inputs are finite; a program needn't handle non-finite values.
Results may differ from the reference program's by a relative error of at most 0.0003.
Values sent between devices are 32-bit elements; how exact they have to be, the bound alone decides.
A program may use at most 128 MiB of HBM per device.

```python
import math
import jax
import jax.numpy as jnp
from jax import lax

NVX = 64
STEPS = 2
NV = 4096
NX = 32
NY = 1024
N_VERT = 2


def draw_cell_type(key, part):
    roll = jax.random.randint(jax.random.fold_in(key, 7), (NX, NY), 0, 10)
    return jnp.where(roll == 0, 1, jnp.where(roll == 1, 2, 0)).astype(jnp.int32)


def level_of(own_key, shape, split, smallest, top_value):
    def one(dim, blocks):
        steps = jax.random.uniform(jax.random.fold_in(jax.random.fold_in(own_key, 6), dim), (blocks,), jnp.float32, smallest / len(split), top_value / len(split))
        return jnp.repeat(jnp.exp(steps), shape[dim] // blocks).reshape((-1,) + (1,) * (len(shape) - dim - 1))

    loudness = one(*split[0])
    for cut in split[1:]:
        loudness = loudness * one(*cut)
    return loudness


def scatter_about(stream_key, shape, width, reach, shards=(), kind=jnp.bfloat16):
    loudness = level_of(stream_key, shape, shards, -0.22, 0.18) if shards else 1.0
    result = jax.random.normal(stream_key, shape, jnp.float32) * width * loudness
    return jnp.minimum(jnp.maximum(result, -reach), reach).astype(kind)


def setup_inputs(seed: int = 0) -> dict:
    arg_keys = jax.random.split(jax.random.key(seed), 5)
    return {
        "distribution": scatter_about(arg_keys[0], (NX, NY, NV), 1.0, 6.0, ((0, 2), (1, 64), (2, 2)), jnp.float32),
        "density": jnp.clip(jnp.exp(math.log(3.0) - 2.3025851 * jax.random.uniform(arg_keys[1], (NX, NY), jnp.float32) ** level_of(arg_keys[1], (NX, NY), ((0, 2), (1, 64)), -0.2, 0.2)), 0.3, 3.0),
        "cell_type": draw_cell_type(jax.random.fold_in(arg_keys[4], 71), 0),
        "inflow": scatter_about(arg_keys[3], (NV,), 1.0, 6.0, ((0, 2),), jnp.float32),
    }


vel_max = 4.0
time_step = 0.1
grad_scale = 2.5
collision_rate = 0.2

def velocity_parts(index):
    spacing = 2.0 * vel_max / NVX
    row_portion = (index // NVX).astype(jnp.float32)
    col_part = (index % NVX).astype(jnp.float32)
    vel_x = (row_portion - 0.5 * (NVX - 1)) * spacing
    vel_y = (col_part - 0.5 * (NVX - 1)) * spacing
    return (vel_x, vel_y)

def kernel_tile(out_index, in_index):
    spacing = 2.0 * vel_max / NVX
    out_x, out_y = velocity_parts(out_index)
    in_x, in_y = velocity_parts(in_index)
    out_sq = out_x * out_x + out_y * out_y
    in_sq = in_x * in_x + in_y * in_y
    diff_sq = (out_x[:, None] - in_x[None, :]) ** 2 + (out_y[:, None] - in_y[None, :]) ** 2 + spacing * spacing
    energy = out_sq[:, None] - in_sq[None, :]
    radius = jnp.sqrt(diff_sq)
    far_part = 2.0 / radius * jnp.exp(-diff_sq / 8.0 - energy * energy / (8.0 * diff_sq))
    near_part = radius * jnp.exp(-(out_sq[:, None] + in_sq[None, :]) / 4.0)
    return grad_scale * spacing * spacing * (far_part - near_part)

def flux_change(strip, courant, axis):
    count = strip.shape[axis] - 4
    diff = lax.slice_in_dim(strip, 1, count + 4, axis=axis) - lax.slice_in_dim(strip, 0, count + 3, axis=axis)
    lower = lax.slice_in_dim(diff, 0, count + 2, axis=axis)
    upper = lax.slice_in_dim(diff, 1, count + 3, axis=axis)
    slope = 0.5 * (jnp.sign(lower) + jnp.sign(upper)) * jnp.minimum(jnp.abs(lower), jnp.abs(upper))
    forward = courant > 0
    upwind = jnp.where(forward, lax.slice_in_dim(strip, 1, count + 2, axis=axis), lax.slice_in_dim(strip, 2, count + 3, axis=axis))
    up_slope = jnp.where(forward, lax.slice_in_dim(slope, 0, count + 1, axis=axis), lax.slice_in_dim(slope, 1, count + 2, axis=axis))
    magnitude = jnp.abs(courant)
    flux = courant * upwind + 0.5 * magnitude * (1.0 - magnitude) * up_slope
    return lax.slice_in_dim(flux, 1, count + 1, axis=axis) - lax.slice_in_dim(flux, 0, count, axis=axis)

def advect(padded, courant_x, courant_y):
    row_term = flux_change(padded[:, 2:-2], courant_x, 0)
    col_term = flux_change(padded[2:-2], courant_y, 1)
    return padded[2:-2, 2:-2] - row_term - col_term

def reference(distribution, density, cell_type, inflow):
    all_index = jnp.arange(NV, dtype=jnp.int32)
    vel_x, vel_y = velocity_parts(all_index)
    courant_x = time_step * vel_x
    courant_y = time_step * vel_y
    collision_frequency = 1.0 + (vel_x * vel_x + vel_y * vel_y) / 8.0
    block_len = NV // N_VERT
    solid_wall_cell = (cell_type == 1)[:, :, None]
    inflow_cell = (cell_type == 2)[:, :, None]
    field = distribution
    for step in range(STEPS):
        padded = jnp.pad(field, ((2, 2), (2, 2), (0, 0)))
        transported_density = advect(padded, courant_x, courant_y)
        rows = transported_density.reshape(NX * NY, NV)

        def block_gain_term(block_id):
            out_index = block_id * block_len + jnp.arange(block_len, dtype=jnp.int32)
            tile = kernel_tile(out_index, all_index)
            return lax.dot_general(rows, tile, (((1,), (1,)), ((), ())), precision=lax.Precision.HIGHEST, preferred_element_type=jnp.float32)
        parts = lax.map(block_gain_term, jnp.arange(N_VERT, dtype=jnp.int32))
        gain_term = jnp.transpose(parts, (1, 0, 2)).reshape(NX, NY, NV)
        post_collision_density = transported_density + collision_rate * density[:, :, None] * (gain_term - collision_frequency * transported_density)
        field = jnp.where(solid_wall_cell, jnp.float32(0.0), jnp.where(inflow_cell, inflow[None, None, :], post_collision_density))
    return field
```

```python
import functools

import jax
import jax.numpy as jnp
from jax import lax
from jax.experimental import pallas as pl
from jax.experimental.pallas import tpu as pltpu
from jax.sharding import PartitionSpec as P

MESH = pl.DeviceIdType.MESH
F32 = jnp.float32
BF16 = jnp.bfloat16

NVX = 64
HALF = 32
STEPS = 2
SPACING = 8.0 / NVX
TIME_STEP = 0.1
COLLISION_RATE = 0.2
GAIN_SCALE = 2.0 * 2.5 * SPACING * SPACING / 4.0
LOG2E = 1.4426950408889634

ROWS = 16
COLS = 16
LOCAL = 2048
PAD_X = ROWS + 4
PAD_Y = 32
TOP = 8


def iota(shape, dim):
    return lax.broadcasted_iota(jnp.int32, shape, dim)


def as_f32(x):
    return x.astype(F32)


def clamp_slope(a, b):
    return jnp.minimum(jnp.maximum(b, jnp.minimum(a, 0.0)), jnp.maximum(a, 0.0))


def split(x):
    hi = x.astype(BF16)
    lo = (x - hi.astype(F32)).astype(BF16)
    return hi, lo


def mm(a, b):
    return jnp.dot(a, b, preferred_element_type=F32)


def parity_maps(h_ref):
    row, col = iota((256, 256), 0), iota((256, 256), 1)
    for k in range(4):
        lane, out = (row, col) if k < 2 else (col, row)
        odd, out_i, b = out // 128, (out // 32) % 4, out % 32
        lane_i, j = lane // 64, lane % 64
        same = lane_i == (out_i if k % 2 == 0 else 3 - out_i)
        upper = (j == HALF + b) & same
        lower = (j == HALF - 1 - b) & same
        value = jnp.where(upper, 1.0, jnp.where(lower, jnp.where(odd == 1, -1.0, 1.0), 0.0))
        h_ref[k] = value.astype(BF16)


def magnitude(i, vt):
    return (jnp.where(vt == 1, as_f32(i), (HALF - 1.0) - as_f32(i)) + 0.5) * SPACING


def make_kernel_blocks(vt, khi, klo):
    qv = (as_f32(iota((32, 128), 1) % 32) + 0.5) * SPACING
    qw = (as_f32(iota((32, 128), 0)) + 0.5) * SPACING
    dy = ((qv - qw) * (qv - qw) + SPACING * SPACING, (qv + qw) * (qv + qw) + SPACING * SPACING)
    ey = qv * qv - qw * qw
    gy = jnp.exp(-(qv * qv + qw * qw) / 4.0) * 0.5
    lane_i = iota((1, 128), 1) // 32

    def tile(t, carry):
        n, i = t // 32, t % 32
        pv = magnitude(n * 4 + lane_i, vt)
        pw = magnitude(jnp.zeros((1, 128), jnp.int32) + i, vt)
        e = ey + (pv * pv - pw * pw)
        e2 = e * e
        g = gy * jnp.exp(-(pv * pv + pw * pw) / 4.0)
        dx = ((pv - pw) * (pv - pw), (pv + pw) * (pv + pw))
        parts = []
        for a in range(2):
            for b in range(2):
                r2 = dy[b] + dx[a]
                rs = lax.rsqrt(r2)
                arg = (r2 + e2 * (rs * rs)) * (-LOG2E / 8.0)
                parts.append(jnp.exp2(arg) * rs - (r2 * rs) * g)
        mm_, mp, pm, pp = parts
        sm, dm = mm_ + mp, mm_ - mp
        sp, dp = pm + pp, pm - pp
        blocks = (sm + sp, dm + dp, sm - sp, dm - dp)
        at = pl.ds(pl.multiple_of(i * 32, 32), 32)
        lanes = pl.ds(pl.multiple_of(n * 128, 128), 128)
        for k in range(4):
            hi, lo = split(blocks[k])
            khi[k, at, lanes] = hi
            klo[k, at, lanes] = lo
        return carry

    lax.fori_loop(0, 256, tile, 0)


def advect(vt, pad, adv):
    lane = iota((1, 128), 1)
    vy = (as_f32(lane % 64) - 0.5 * (NVX - 1)) * SPACING
    ay = TIME_STEP * jnp.abs(vy)
    cy = 0.5 * ay * (1.0 - ay)
    forward = jnp.broadcast_to(vy > 0, (COLS, 128))
    sign = 2 * vt - 1
    first = 2 + (1 - vt) * (ROWS - 1)

    def chunk(m, carry):
        lanes = pl.ds(pl.multiple_of(m * 128, 128), 128)
        index = vt * HALF + m * 2 + lane // 64
        ax = TIME_STEP * jnp.abs((as_f32(index) - 0.5 * (NVX - 1)) * SPACING)
        cx = 0.5 * ax * (1.0 - ax)

        def row(px):
            return pad[px, TOP:TOP + COLS, lanes]

        u2, u1 = row(first - 2 * sign), row(first - sign)
        here = row(first)
        d0 = here - u1
        s1 = clamp_slope(u1 - u2, d0)
        for k in range(ROWS):
            px = first + k * sign
            ahead = row(px + sign)
            dw = ahead - here
            s0 = clamp_slope(d0, dw)
            term_x = ax * d0 + cx * (s0 - s1)
            l1 = pad[px, TOP - 1:TOP - 1 + COLS, lanes]
            l2 = pad[px, TOP - 2:TOP - 2 + COLS, lanes]
            r1 = pad[px, TOP + 1:TOP + 1 + COLS, lanes]
            r2 = pad[px, TOP + 2:TOP + 2 + COLS, lanes]
            v1 = jnp.where(forward, l1, r1)
            v2 = jnp.where(forward, l2, r2)
            w1 = jnp.where(forward, r1, l1)
            e0 = here - v1
            t0 = clamp_slope(e0, w1 - here)
            t1 = clamp_slope(v1 - v2, e0)
            term_y = ay * e0 + cy * (t0 - t1)
            out = here - term_x - term_y
            x = px - 2
            adv[0, x, :, lanes] = out[:8]
            adv[1, x, :, lanes] = out[8:]
            here, d0, s1 = ahead, dw, s0
        return carry

    lax.fori_loop(0, LOCAL // 128, chunk, 0)


def flat(ref):
    return ref.reshape(128, LOCAL)


def to_parities(own, other, h_ref, s_ref):
    own, other = flat(own), flat(other)

    def chunk(n, carry):
        hi, lo = split(own[:, pl.ds(pl.multiple_of(n * 256, 256), 256)])
        y = mm(hi, h_ref[0]) + mm(lo, h_ref[0])
        hi, lo = split(other[:, pl.ds(pl.multiple_of((7 - n) * 256, 256), 256)])
        z = mm(hi, h_ref[1]) + mm(lo, h_ref[1])
        lanes = pl.ds(pl.multiple_of(n * 128, 128), 128)
        for k, value in enumerate((y + z, y - z)):
            hi, lo = split(value)
            for odd in range(2):
                s_ref[2 * k + odd, :128, lanes] = hi[:, 128 * odd:128 * odd + 128]
                s_ref[2 * k + odd, 128:, lanes] = lo[:, 128 * odd:128 * odd + 128]
        return carry

    lax.fori_loop(0, 8, chunk, 0)


def contract(s_ref, khi, klo, g_ref):
    def tile(t, carry):
        k, n = t // 4, t % 4
        lanes = pl.ds(pl.multiple_of(n * 256, 256), 256)
        both = mm(s_ref[k], khi[k, :, lanes])
        rest = mm(s_ref[k, :128, :], klo[k, :, lanes])
        g_ref[k, :, lanes] = both[:128] + both[128:] + rest
        return carry

    lax.fori_loop(0, 16, tile, 0)


def from_parities(g_ref, h_ref, own, other):
    own, other = flat(own), flat(other)

    def chunk(n, carry):
        lanes = pl.ds(pl.multiple_of(n * 128, 128), 128)
        even = jnp.concatenate([g_ref[0, :, lanes], g_ref[1, :, lanes]], axis=1)
        odd = jnp.concatenate([g_ref[2, :, lanes], g_ref[3, :, lanes]], axis=1)
        hi, lo = split(even + odd)
        own[:, pl.ds(pl.multiple_of(n * 256, 256), 256)] = mm(hi, h_ref[2]) + mm(lo, h_ref[2])
        hi, lo = split(even - odd)
        other[:, pl.ds(pl.multiple_of((7 - n) * 256, 256), 256)] = mm(hi, h_ref[3]) + mm(lo, h_ref[3])
        return carry

    lax.fori_loop(0, 8, chunk, 0)


def collide(vt, adv, gains, dens_b, type_b, inflow, put):
    lane = iota((1, 128), 1)
    vy = (as_f32(lane % 64) - 0.5 * (NVX - 1)) * SPACING

    def chunk(m, carry):
        lanes = pl.ds(pl.multiple_of(m * 128, 128), 128)
        index = vt * HALF + m * 2 + lane // 64
        vx = (as_f32(index) - 0.5 * (NVX - 1)) * SPACING
        nu = 1.0 + (vx * vx + vy * vy) / 8.0
        held = inflow[:, lanes]
        for x in range(ROWS):
            for half in range(2):
                a = adv[half, x, :, lanes]
                gain = gains[half, x, :, lanes] * GAIN_SCALE
                rate = dens_b[x, 8 * half:8 * half + 8, :]
                kind = type_b[x, 8 * half:8 * half + 8, :]
                after = a + rate * (gain - nu * a)
                after = jnp.where(kind == 1, 0.0, jnp.where(kind == 2, held, after))
                put(x, half, lanes, after)
        return carry

    lax.fori_loop(0, LOCAL // 128, chunk, 0)


def kernel(dist, density, cell_type, inflow, out, pads, packs, halos, adv, fin, gains, gsend, s_ref, g_ref,
           khi, klo, h_ref, dens_b, type_b, load_sem, xsend, xrecv, ysend, yrecv, fsend, frecv, qsend, qrecv):
    gx, gy, vt = lax.axis_index("gx"), lax.axis_index("gy"), lax.axis_index("vert")
    last = lax.axis_size("gy") - 1
    has_left, has_right = gy > 0, gy < last
    gets_two = gx == vt

    load = pltpu.make_async_copy(dist, pads.at[0, pl.ds(2, ROWS), pl.ds(TOP, COLS), :], load_sem)
    load.start()

    barrier = pltpu.get_barrier_semaphore()
    pl.semaphore_signal(barrier, inc=1, device_id=(1 - gx, gy, vt), device_id_type=MESH)
    pl.semaphore_signal(barrier, inc=1, device_id=(gx, gy, 1 - vt), device_id_type=MESH)

    @pl.when(has_left)
    def _():
        pl.semaphore_signal(barrier, inc=1, device_id=(gx, gy - 1, vt), device_id_type=MESH)

    @pl.when(has_right)
    def _():
        pl.semaphore_signal(barrier, inc=1, device_id=(gx, gy + 1, vt), device_id_type=MESH)

    pl.semaphore_wait(barrier, 2 + has_left.astype(jnp.int32) + has_right.astype(jnp.int32))

    def x_copy(step, count):
        if count == 2:
            start, to = (1 - gx) * (ROWS - 2), gx * (ROWS + 2)
        else:
            start, to = (1 - gx) * (ROWS - 1), 1 + gx * (ROWS + 1)
        return pltpu.make_async_remote_copy(
            src_ref=pads.at[step, pl.ds(2 + start, count), pl.ds(TOP, COLS), :],
            dst_ref=pads.at[step, pl.ds(to, count), pl.ds(TOP, COLS), :],
            send_sem=xsend.at[step], recv_sem=xrecv.at[step],
            device_id=(1 - gx, gy, vt), device_id_type=MESH)

    def y_copy(step, side):
        return pltpu.make_async_remote_copy(
            src_ref=packs.at[step, side], dst_ref=halos.at[step, 1 - side],
            send_sem=ysend.at[step, side], recv_sem=yrecv.at[step, 1 - side],
            device_id=(gx, gy - 1 + 2 * side, vt), device_id_type=MESH)

    def y_wait(step, side):
        return pltpu.make_async_remote_copy(
            src_ref=packs.at[step, side], dst_ref=halos.at[step, side],
            send_sem=ysend.at[step, side], recv_sem=yrecv.at[step, side],
            device_id=(gx, gy - 1 + 2 * side, vt), device_id_type=MESH)

    def x_wait(step, count):
        if count == 2:
            to = (1 - gx) * (ROWS + 2)
        else:
            to = 1 + (1 - gx) * (ROWS + 1)
        return pltpu.make_async_remote_copy(
            src_ref=pads.at[step, pl.ds(to, count), pl.ds(TOP, COLS), :],
            dst_ref=pads.at[step, pl.ds(to, count), pl.ds(TOP, COLS), :],
            send_sem=xsend.at[step], recv_sem=xrecv.at[step],
            device_id=(1 - gx, gy, vt), device_id_type=MESH)

    def send_halos(step):
        @pl.when(gets_two)
        def _():
            x_copy(step, 1).start()

        @pl.when(jnp.logical_not(gets_two))
        def _():
            x_copy(step, 2).start()

        for side, present in ((0, has_left), (1, has_right)):
            y = TOP + side * (COLS - 2)
            for x in range(ROWS):
                at = 2 * (x % 4)
                packs[step, side, x // 4, at:at + 2, :] = pads[step, 2 + x, y:y + 2, :]
            pl.when(present)(lambda side=side: y_copy(step, side).start())

    def clear_missing(step):
        zero_row = jnp.zeros((COLS, LOCAL), F32)

        @pl.when(gets_two)
        def _():
            pads[step, 1 + (1 - vt) * 0 + vt * (ROWS + 1), pl.ds(TOP, COLS), :] = zero_row

        @pl.when(jnp.logical_not(gets_two))
        def _():
            for k in range(2):
                pads[step, (1 - vt) * (ROWS + 2) + k, pl.ds(TOP, COLS), :] = zero_row

        for side, present in ((0, has_left), (1, has_right)):
            @pl.when(jnp.logical_not(present))
            def _():
                for group in range(4):
                    halos[step, side, group] = jnp.zeros((8, LOCAL), F32)

    def take_halos(step):
        @pl.when(gets_two)
        def _():
            x_wait(step, 2).wait_recv()

        @pl.when(jnp.logical_not(gets_two))
        def _():
            x_wait(step, 1).wait_recv()

        for side, present in ((0, has_left), (1, has_right)):
            pl.when(present)(lambda side=side: y_wait(step, side).wait_recv())
            y = TOP - 2 + side * (COLS + 2)
            for x in range(ROWS):
                at = 2 * (x % 4)
                pads[step, 2 + x, y:y + 2, :] = halos[step, side, x // 4, at:at + 2, :]

    def wait_sent(step):
        @pl.when(gets_two)
        def _():
            x_copy(step, 1).wait_send()

        @pl.when(jnp.logical_not(gets_two))
        def _():
            x_copy(step, 2).wait_send()

        for side, present in ((0, has_left), (1, has_right)):
            pl.when(present)(lambda side=side: y_copy(step, side).wait_send())

    def partner_copy(src, dst, step, send, recv):
        return pltpu.make_async_remote_copy(
            src_ref=src, dst_ref=dst, send_sem=send.at[step], recv_sem=recv.at[step],
            device_id=(gx, gy, 1 - vt), device_id_type=MESH)

    load.wait()
    send_halos(0)
    for step in range(STEPS):
        clear_missing(step)
    rate = (COLLISION_RATE * density[...]).T
    kind = as_f32(cell_type[...]).T
    for x in range(ROWS):
        dens_b[x] = jnp.broadcast_to(rate[:, x:x + 1], (COLS, 128))
        type_b[x] = jnp.broadcast_to(kind[:, x:x + 1], (COLS, 128))
    parity_maps(h_ref)
    make_kernel_blocks(vt, khi, klo)

    for step in range(STEPS):
        take_halos(step)
        advect(vt, pads.at[step], adv)
        there = partner_copy(adv.at[1 - vt], fin.at[step], step, fsend, frecv)
        there.start()
        there.wait()
        to_parities(adv.at[vt], fin.at[step], h_ref, s_ref)
        contract(s_ref, khi, klo, g_ref)
        from_parities(g_ref, h_ref, gains.at[step, vt], gsend.at[step])
        back = partner_copy(gsend.at[step], gains.at[step, vt], step, qsend, qrecv)
        back.start()
        partner_copy(gsend.at[step], gains.at[step, 1 - vt], step, qsend, qrecv).wait_recv()
        back.wait_send()
        if step < STEPS - 1:
            def put(x, half, lanes, value):
                pads[step + 1, 2 + x, TOP + 8 * half:TOP + 8 * half + 8, lanes] = value
        else:
            def put(x, half, lanes, value):
                out[x, 8 * half:8 * half + 8, lanes] = value
        collide(vt, adv, gains.at[step], dens_b, type_b, inflow, put)
        wait_sent(step)
        if step < STEPS - 1:
            send_halos(step + 1)


def per_device(distribution, density, cell_type, inflow):
    vmem = pl.BlockSpec(memory_space=pltpu.VMEM)
    dma = pltpu.SemaphoreType.DMA
    return pl.pallas_call(
        kernel,
        out_shape=jax.ShapeDtypeStruct((ROWS, COLS, LOCAL), F32),
        in_specs=[pl.BlockSpec(memory_space=pl.ANY), vmem, vmem, vmem],
        out_specs=vmem,
        scratch_shapes=[
            pltpu.VMEM((STEPS, PAD_X, PAD_Y, LOCAL), F32),
            pltpu.VMEM((STEPS, 2, 4, 8, LOCAL), F32),
            pltpu.VMEM((STEPS, 2, 4, 8, LOCAL), F32),
            pltpu.VMEM((2, ROWS, 8, LOCAL), F32),
            pltpu.VMEM((STEPS, ROWS, 8, LOCAL), F32),
            pltpu.VMEM((STEPS, 2, ROWS, 8, LOCAL), F32),
            pltpu.VMEM((STEPS, ROWS, 8, LOCAL), F32),
            pltpu.VMEM((4, 256, 1024), BF16),
            pltpu.VMEM((4, 128, 1024), F32),
            pltpu.VMEM((4, 1024, 1024), BF16),
            pltpu.VMEM((4, 1024, 1024), BF16),
            pltpu.VMEM((4, 256, 256), BF16),
            pltpu.VMEM((ROWS, COLS, 128), F32),
            pltpu.VMEM((ROWS, COLS, 128), F32),
            dma,
            dma((STEPS,)), dma((STEPS,)),
            dma((STEPS, 2)), dma((STEPS, 2)),
            dma((STEPS,)), dma((STEPS,)),
            dma((STEPS,)), dma((STEPS,)),
        ],
        compiler_params=pltpu.CompilerParams(
            collective_id=0, has_side_effects=True, vmem_limit_bytes=67000000),
    )(distribution, density, cell_type, inflow.reshape(1, LOCAL))


def solution(mesh):
    placed = (P("gx", "gy", "vert"), P("gx", "gy"), P("gx", "gy"), P("vert"))
    return jax.shard_map(
        per_device, mesh=mesh, in_specs=placed, out_specs=P("gx", "gy", "vert"), check_vma=False
    )
```

```python
import functools

import jax
import jax.numpy as jnp
from jax import lax
from jax.experimental import pallas as pl
from jax.experimental.pallas import tpu as pltpu
from jax.sharding import PartitionSpec as P

MESH = pl.DeviceIdType.MESH
F32 = jnp.float32
BF16 = jnp.bfloat16

NVX = 64
HALF = 32
STEPS = 2
SPACING = 8.0 / NVX
TIME_STEP = 0.1
COLLISION_RATE = 0.2
GAIN_SCALE = 2.0 * 2.5 * SPACING * SPACING / 4.0
LOG2E = 1.4426950408889634

ROWS = 16
COLS = 16
GROUP = 8
CELLS = GROUP * COLS
LOCAL = 2048
PAD_X = ROWS + 4
PAD_Y = 32
TOP = 8


def iota(shape, dim):
    return lax.broadcasted_iota(jnp.int32, shape, dim)


def as_f32(x):
    return x.astype(F32)


def clamp_slope(a, b):
    return jnp.minimum(jnp.maximum(b, jnp.minimum(a, 0.0)), jnp.maximum(a, 0.0))


def split(x):
    hi = x.astype(BF16)
    lo = (x - hi.astype(F32)).astype(BF16)
    return hi, lo


def mm(a, b):
    return jnp.dot(a, b, preferred_element_type=F32)


def parity_maps(vt, h_ref):
    row, col = iota((256, 256), 0), iota((256, 256), 1)
    for k, (lane, out) in enumerate(((row, col), (col, row))):
        odd, out_i, b = out // 128, (out // 32) % 4, out % 32
        lane_i, j = lane // 64, lane % 64
        same = lane_i == jnp.where(vt == 1, out_i, 3 - out_i)
        upper = (j == HALF + b) & same
        lower = (j == HALF - 1 - b) & same
        value = jnp.where(upper, 1.0, jnp.where(lower, jnp.where(odd == 1, -1.0, 1.0), 0.0))
        h_ref[k] = value.astype(BF16)


def magnitude(i):
    return (as_f32(i) + 0.5) * SPACING


def make_kernel_blocks(vt, khi, klo):
    qv = (as_f32(iota((32, 128), 1) % 32) + 0.5) * SPACING
    qw = (as_f32(iota((32, 128), 0)) + 0.5) * SPACING
    dy = ((qv - qw) * (qv - qw) + SPACING * SPACING, (qv + qw) * (qv + qw) + SPACING * SPACING)
    ey = qv * qv - qw * qw
    gy = jnp.exp(-(qv * qv + qw * qw) / 4.0) * 0.5
    lane_i = iota((1, 128), 1) // 32
    sign = as_f32(1 - 2 * vt)

    def tile(t, carry):
        n, i = t // 32, t % 32
        pv = magnitude(n * 4 + lane_i)
        pw = magnitude(jnp.zeros((1, 128), jnp.int32) + i)
        e = ey + (pv * pv - pw * pw)
        e2 = e * e
        g = gy * jnp.exp(-(pv * pv + pw * pw) / 4.0)
        dx = ((pv - pw) * (pv - pw), (pv + pw) * (pv + pw))
        parts = []
        for a in range(2):
            for b in range(2):
                r2 = dy[b] + dx[a]
                rs = lax.rsqrt(r2)
                arg = (r2 + e2 * (rs * rs)) * (-LOG2E / 8.0)
                parts.append(jnp.exp2(arg) * rs - (r2 * rs) * g)
        mm_, mp, pm, pp = parts
        sm, dm = mm_ + mp, mm_ - mp
        sp, dp = pm + pp, pm - pp
        blocks = (sm + sign * sp, dm + sign * dp)
        at = pl.ds(pl.multiple_of(i * 32, 32), 32)
        lanes = pl.ds(pl.multiple_of(n * 128, 128), 128)
        for k in range(2):
            hi, lo = split(blocks[k])
            khi[k, at, lanes] = hi
            klo[k, at, lanes] = lo
        return carry

    lax.fori_loop(0, 256, tile, 0)


def advect(vt, pad, base, adv):
    lane = iota((1, 128), 1)
    vy = (as_f32(lane % 64) - 0.5 * (NVX - 1)) * SPACING
    ay = TIME_STEP * jnp.abs(vy)
    cy = 0.5 * ay * (1.0 - ay)
    forward = jnp.broadcast_to(vy > 0, (COLS, 128))
    sign = 2 * vt - 1
    offset = (1 - vt) * (GROUP - 1)
    first = 2 + base + offset

    def chunk(m, carry):
        lanes = pl.ds(pl.multiple_of(m * 128, 128), 128)
        index = vt * HALF + m * 2 + lane // 64
        ax = TIME_STEP * jnp.abs((as_f32(index) - 0.5 * (NVX - 1)) * SPACING)
        cx = 0.5 * ax * (1.0 - ax)

        def row(px):
            return pad[px, TOP:TOP + COLS, lanes]

        u2, u1 = row(first - 2 * sign), row(first - sign)
        here = row(first)
        d0 = here - u1
        s1 = clamp_slope(u1 - u2, d0)
        for k in range(GROUP):
            px = first + k * sign
            ahead = row(px + sign)
            dw = ahead - here
            s0 = clamp_slope(d0, dw)
            term_x = ax * d0 + cx * (s0 - s1)
            l1 = pad[px, TOP - 1:TOP - 1 + COLS, lanes]
            l2 = pad[px, TOP - 2:TOP - 2 + COLS, lanes]
            r1 = pad[px, TOP + 1:TOP + 1 + COLS, lanes]
            r2 = pad[px, TOP + 2:TOP + 2 + COLS, lanes]
            v1 = jnp.where(forward, l1, r1)
            v2 = jnp.where(forward, l2, r2)
            w1 = jnp.where(forward, r1, l1)
            e0 = here - v1
            t0 = clamp_slope(e0, w1 - here)
            t1 = clamp_slope(v1 - v2, e0)
            term_y = ay * e0 + cy * (t0 - t1)
            adv[offset + k * sign, :, lanes] = here - term_x - term_y
            here, d0, s1 = ahead, dw, s0
        return carry

    lax.fori_loop(0, LOCAL // 128, chunk, 0)


def wide(n):
    return pl.ds(pl.multiple_of(n * 256, 256), 256)


def stack(n, value, t_ref):
    hi, lo = split(value)
    t_ref[128 * n:128 * n + 128, :] = hi
    t_ref[1024 + 128 * n:1024 + 128 * n + 128, :] = lo


def to_parities(vt, adv, h_ref, t_ref, y_ref):
    cells = adv.reshape(CELLS, LOCAL)
    for n in range(8):
        stack(n, cells[:, wide(jnp.where(vt == 1, n, 7 - n))], t_ref)
    y = mm(t_ref[...], h_ref[0])
    for n in range(8):
        value = y[128 * n:128 * n + 128] + y[1024 + 128 * n:1024 + 128 * n + 128]
        for odd in range(2):
            y_ref[odd, :, 128 * n:128 * n + 128] = value[:, 128 * odd:128 * odd + 128]


def contract(vt, own, other, khi, klo, g_ref):
    sign = as_f32(1 - 2 * vt)
    for k in range(2):
        hi, lo = split(own[k] + sign * other[k])
        both = mm(jnp.concatenate([hi, lo], axis=0), khi[k])
        g_ref[k] = both[:CELLS] + both[CELLS:] + mm(hi, klo[k])


def from_parities(vt, own, other, h_ref, t_ref, adv, dens, kinds, inflow, put):
    sign = as_f32(2 * vt - 1)
    cells = adv.reshape(CELLS, LOCAL)
    for n in range(8):
        at = slice(128 * n, 128 * n + 128)
        stack(n, jnp.concatenate([own[k, :, at] + sign * other[k, :, at] for k in range(2)], axis=1), t_ref)
    back = mm(t_ref[...], h_ref[1])
    lane = iota((1, 256), 1)
    vy = (as_f32(lane % 64) - 0.5 * (NVX - 1)) * SPACING
    rate, kind = (jnp.concatenate([ref[...]] * 2, axis=1) for ref in (dens, kinds))
    for n in range(8):
        m = jnp.where(vt == 1, n, 7 - n)
        gain = (back[128 * n:128 * n + 128] + back[1024 + 128 * n:1024 + 128 * n + 128]) * GAIN_SCALE
        vx = (as_f32(vt * HALF + m * 4 + lane // 64) - 0.5 * (NVX - 1)) * SPACING
        nu = 1.0 + (vx * vx + vy * vy) / 8.0
        a = cells[:, wide(m)]
        after = a + rate * (gain - nu * a)
        after = jnp.where(kind == 1, 0.0, jnp.where(kind == 2, inflow[:, wide(m)], after))
        put(wide(m), after.reshape(GROUP, COLS, 256))


def kernel(dist, density, cell_type, inflow, out, pads, packs, halos, adv, yown, yin, gown, gin, t_ref,
           khi, klo, h_ref, dens_b, type_b, load_sem, xsend, xrecv, ysend, yrecv, fsend, frecv, qsend, qrecv):
    gx, gy, vt = lax.axis_index("gx"), lax.axis_index("gy"), lax.axis_index("vert")
    last = lax.axis_size("gy") - 1
    has_left, has_right = gy > 0, gy < last
    gets_two = gx == vt
    sides = ((0, has_left), (1, has_right))
    bases = ((1 - gx) * GROUP, gx * GROUP)

    load = pltpu.make_async_copy(dist, pads.at[0, pl.ds(2, ROWS), pl.ds(TOP, COLS), :], load_sem)
    load.start()

    barrier = pltpu.get_barrier_semaphore()
    pl.semaphore_signal(barrier, inc=1, device_id=(1 - gx, gy, vt), device_id_type=MESH)
    pl.semaphore_signal(barrier, inc=1, device_id=(gx, gy, 1 - vt), device_id_type=MESH)

    @pl.when(has_left)
    def _():
        pl.semaphore_signal(barrier, inc=1, device_id=(gx, gy - 1, vt), device_id_type=MESH)

    @pl.when(has_right)
    def _():
        pl.semaphore_signal(barrier, inc=1, device_id=(gx, gy + 1, vt), device_id_type=MESH)

    def x_copy(step, count):
        if count == 2:
            start, to = (1 - gx) * (ROWS - 2), gx * (ROWS + 2)
        else:
            start, to = (1 - gx) * (ROWS - 1), 1 + gx * (ROWS + 1)
        return pltpu.make_async_remote_copy(
            src_ref=pads.at[step, pl.ds(2 + start, count), pl.ds(TOP, COLS), :],
            dst_ref=pads.at[step, pl.ds(to, count), pl.ds(TOP, COLS), :],
            send_sem=xsend.at[step], recv_sem=xrecv.at[step],
            device_id=(1 - gx, gy, vt), device_id_type=MESH)

    def x_wait(step, count):
        if count == 2:
            to = (1 - gx) * (ROWS + 2)
        else:
            to = 1 + (1 - gx) * (ROWS + 1)
        return pltpu.make_async_remote_copy(
            src_ref=pads.at[step, pl.ds(to, count), pl.ds(TOP, COLS), :],
            dst_ref=pads.at[step, pl.ds(to, count), pl.ds(TOP, COLS), :],
            send_sem=xsend.at[step], recv_sem=xrecv.at[step],
            device_id=(1 - gx, gy, vt), device_id_type=MESH)

    def y_copy(step, group, side, to):
        return pltpu.make_async_remote_copy(
            src_ref=packs.at[step, group, side], dst_ref=halos.at[step, group, to],
            send_sem=ysend.at[step, group, side], recv_sem=yrecv.at[step, group, to],
            device_id=(gx, gy - 1 + 2 * side, vt), device_id_type=MESH)

    def send_x(step):
        pl.when(gets_two)(lambda: x_copy(step, 1).start())
        pl.when(jnp.logical_not(gets_two))(lambda: x_copy(step, 2).start())

    def send_y(step, group):
        for side, present in sides:
            y = TOP + side * (COLS - 2)
            for x in range(GROUP):
                at = 2 * (x % 4)
                packs[step, group, side, x // 4, at:at + 2, :] = pads[step, 2 + bases[group] + x, y:y + 2, :]
            pl.when(present)(lambda side=side: y_copy(step, group, side, 1 - side).start())

    def clear_missing(step):
        zero_row = jnp.zeros((COLS, LOCAL), F32)

        @pl.when(gets_two)
        def _():
            pads[step, 1 + vt * (ROWS + 1), pl.ds(TOP, COLS), :] = zero_row

        @pl.when(jnp.logical_not(gets_two))
        def _():
            for k in range(2):
                pads[step, (1 - vt) * (ROWS + 2) + k, pl.ds(TOP, COLS), :] = zero_row

        for side, present in sides:
            @pl.when(jnp.logical_not(present))
            def _():
                for group in range(2):
                    for part in range(2):
                        halos[step, group, side, part] = jnp.zeros((8, LOCAL), F32)

    def take_x(step):
        pl.when(gets_two)(lambda: x_wait(step, 2).wait_recv())
        pl.when(jnp.logical_not(gets_two))(lambda: x_wait(step, 1).wait_recv())

    def take_y(step, group):
        for side, present in sides:
            pl.when(present)(lambda side=side: y_copy(step, group, side, side).wait_recv())
            y = TOP - 2 + side * (COLS + 2)
            for x in range(GROUP):
                at = 2 * (x % 4)
                pads[step, 2 + bases[group] + x, y:y + 2, :] = halos[step, group, side, x // 4, at:at + 2, :]

    def wait_sent(step):
        pl.when(gets_two)(lambda: x_copy(step, 1).wait_send())
        pl.when(jnp.logical_not(gets_two))(lambda: x_copy(step, 2).wait_send())
        for group in range(2):
            for side, present in sides:
                pl.when(present)(lambda side=side, group=group: y_copy(step, group, side, side).wait_send())

    def partner_copy(src, dst, send, recv, step, group):
        return pltpu.make_async_remote_copy(
            src_ref=src.at[step, group], dst_ref=dst.at[step, group],
            send_sem=send.at[step, group], recv_sem=recv.at[step, group],
            device_id=(gx, gy, 1 - vt), device_id_type=MESH)

    def there(step, group):
        return partner_copy(yown, yin, fsend, frecv, step, group)

    def back(step, group):
        return partner_copy(gown, gin, qsend, qrecv, step, group)

    def stage_a(step, group):
        advect(vt, pads.at[step], bases[group], adv.at[group])

    def stage_t(step, group):
        to_parities(vt, adv.at[group], h_ref, t_ref, yown.at[step, group])
        there(step, group).start()

    def stage_c(step, group):
        there(step, group).wait_recv()
        contract(vt, yown.at[step, group], yin.at[step, group], khi, klo, gown.at[step, group])
        back(step, group).start()

    def stage_f(step, group):
        back(step, group).wait_recv()
        base = bases[group]
        if step < STEPS - 1:
            def put(lanes, value):
                pads[step + 1, pl.ds(2 + base, GROUP), TOP:TOP + COLS, lanes] = value
        else:
            def put(lanes, value):
                out[pl.ds(base, GROUP), :, lanes] = value
        cells = pl.ds(pl.multiple_of(base * COLS, CELLS), CELLS)
        from_parities(vt, gown.at[step, group], gin.at[step, group], h_ref, t_ref, adv.at[group],
                      dens_b.at[cells], type_b.at[cells], inflow, put)

    load.wait()
    pl.semaphore_wait(barrier, 2 + has_left.astype(jnp.int32) + has_right.astype(jnp.int32))
    send_x(0)
    for group in range(2):
        send_y(0, group)
    for step in range(STEPS):
        clear_missing(step)
    rate = (COLLISION_RATE * density[...]).T
    kind = as_f32(cell_type[...]).T
    for x in range(ROWS):
        dens_b[x * COLS:x * COLS + COLS] = jnp.broadcast_to(rate[:, x:x + 1], (COLS, 128))
        type_b[x * COLS:x * COLS + COLS] = jnp.broadcast_to(kind[:, x:x + 1], (COLS, 128))
    parity_maps(vt, h_ref)
    make_kernel_blocks(vt, khi, klo)

    take_y(0, 1)
    stage_a(0, 1)
    take_y(0, 0)
    take_x(0)
    stage_a(0, 0)
    stage_t(0, 0)
    stage_t(0, 1)
    stage_c(0, 0)
    stage_c(0, 1)
    stage_f(0, 0)
    send_x(1)
    send_y(1, 0)
    stage_f(0, 1)
    send_y(1, 1)
    take_y(1, 1)
    stage_a(1, 1)
    stage_t(1, 1)
    stage_c(1, 1)
    take_y(1, 0)
    take_x(1)
    stage_a(1, 0)
    stage_t(1, 0)
    stage_f(1, 1)
    stage_c(1, 0)
    stage_f(1, 0)
    for step in range(STEPS):
        wait_sent(step)
        for group in range(2):
            there(step, group).wait_send()
            back(step, group).wait_send()


def per_device(distribution, density, cell_type, inflow):
    vmem = pl.BlockSpec(memory_space=pltpu.VMEM)
    dma = pltpu.SemaphoreType.DMA
    pair = pltpu.VMEM((STEPS, 2, 2, CELLS, 1024), F32)
    return pl.pallas_call(
        kernel,
        out_shape=jax.ShapeDtypeStruct((ROWS, COLS, LOCAL), F32),
        in_specs=[pl.BlockSpec(memory_space=pl.ANY), vmem, vmem, vmem],
        out_specs=vmem,
        scratch_shapes=[
            pltpu.VMEM((STEPS, PAD_X, PAD_Y, LOCAL), F32),
            pltpu.VMEM((STEPS, 2, 2, 2, 8, LOCAL), F32),
            pltpu.VMEM((STEPS, 2, 2, 2, 8, LOCAL), F32),
            pltpu.VMEM((2, GROUP, COLS, LOCAL), F32),
            pair, pair, pair, pair,
            pltpu.VMEM((2048, 256), BF16),
            pltpu.VMEM((2, 1024, 1024), BF16),
            pltpu.VMEM((2, 1024, 1024), BF16),
            pltpu.VMEM((2, 256, 256), BF16),
            pltpu.VMEM((ROWS * COLS, 128), F32),
            pltpu.VMEM((ROWS * COLS, 128), F32),
            dma,
            dma((STEPS,)), dma((STEPS,)),
            dma((STEPS, 2, 2)), dma((STEPS, 2, 2)),
            dma((STEPS, 2)), dma((STEPS, 2)),
            dma((STEPS, 2)), dma((STEPS, 2)),
        ],
        compiler_params=pltpu.CompilerParams(
            collective_id=0, has_side_effects=True, vmem_limit_bytes=67000000),
    )(distribution, density, cell_type, inflow.reshape(1, LOCAL))


def solution(mesh):
    placed = (P("gx", "gy", "vert"), P("gx", "gy"), P("gx", "gy"), P("vert"))
    return jax.shard_map(
        per_device, mesh=mesh, in_specs=placed, out_specs=P("gx", "gy", "vert"), check_vma=False
    )
```

```python
import functools

import jax
import jax.numpy as jnp
from jax import lax
from jax.experimental import pallas as pl
from jax.experimental.pallas import tpu as pltpu
from jax.sharding import PartitionSpec as P

MESH = pl.DeviceIdType.MESH
F32 = jnp.float32
BF16 = jnp.bfloat16

NVX = 64
HALF = 32
STEPS = 2
SPACING = 8.0 / NVX
TIME_STEP = 0.1
COLLISION_RATE = 0.2
GAIN_SCALE = 2.0 * 2.5 * SPACING * SPACING / 4.0
LOG2E = 1.4426950408889634

ROWS = 16
COLS = 16
GROUP = 8
CELLS = GROUP * COLS
LOCAL = 2048
PAD_X = ROWS + 4
PAD_Y = 32
TOP = 8


def iota(shape, dim):
    return lax.broadcasted_iota(jnp.int32, shape, dim)


def as_f32(x):
    return x.astype(F32)


def clamp_slope(a, b):
    return jnp.minimum(jnp.maximum(b, jnp.minimum(a, 0.0)), jnp.maximum(a, 0.0))


def split(x):
    hi = x.astype(BF16)
    lo = (x - hi.astype(F32)).astype(BF16)
    return hi, lo


def mm(a, b):
    return jnp.dot(a, b, preferred_element_type=F32)


def parity_maps(vt, h_ref):
    row, col = iota((256, 256), 0), iota((256, 256), 1)
    for k, (lane, out) in enumerate(((row, col), (col, row))):
        odd, out_i, b = out // 128, (out // 32) % 4, out % 32
        lane_i, j = lane // 64, lane % 64
        same = lane_i == jnp.where(vt == 1, out_i, 3 - out_i)
        upper = (j == HALF + b) & same
        lower = (j == HALF - 1 - b) & same
        value = jnp.where(upper, 1.0, jnp.where(lower, jnp.where(odd == 1, -1.0, 1.0), 0.0))
        h_ref[k] = value.astype(BF16)


def magnitude(i):
    return (as_f32(i) + 0.5) * SPACING


def make_kernel_blocks(vt, khi, klo):
    qv = (as_f32(iota((32, 128), 1) % 32) + 0.5) * SPACING
    qw = (as_f32(iota((32, 128), 0)) + 0.5) * SPACING
    dy = ((qv - qw) * (qv - qw) + SPACING * SPACING, (qv + qw) * (qv + qw) + SPACING * SPACING)
    ey = qv * qv - qw * qw
    gy = jnp.exp(-(qv * qv + qw * qw) / 4.0) * 0.5
    lane_i = iota((1, 128), 1) // 32
    sign = as_f32(1 - 2 * vt)

    def tile(t, carry):
        n, i = t // 32, t % 32
        pv = magnitude(n * 4 + lane_i)
        pw = magnitude(jnp.zeros((1, 128), jnp.int32) + i)
        e = ey + (pv * pv - pw * pw)
        e2 = e * e
        g = gy * jnp.exp(-(pv * pv + pw * pw) / 4.0)
        dx = ((pv - pw) * (pv - pw), (pv + pw) * (pv + pw))
        parts = []
        for a in range(2):
            for b in range(2):
                r2 = dy[b] + dx[a]
                rs = lax.rsqrt(r2)
                arg = (r2 + e2 * (rs * rs)) * (-LOG2E / 8.0)
                parts.append(jnp.exp2(arg) * rs - (r2 * rs) * g)
        mm_, mp, pm, pp = parts
        sm, dm = mm_ + mp, mm_ - mp
        sp, dp = pm + pp, pm - pp
        blocks = (sm + sign * sp, dm + sign * dp)
        at = pl.ds(pl.multiple_of(i * 32, 32), 32)
        lanes = pl.ds(pl.multiple_of(n * 128, 128), 128)
        for k in range(2):
            hi, lo = split(blocks[k])
            khi[k, at, lanes] = hi
            klo[k, at, lanes] = lo
        return carry

    lax.fori_loop(0, 256, tile, 0)


def advect(vt, pad, base, start, count, adv):
    lane = iota((1, 128), 1)
    vy = (as_f32(lane % 64) - 0.5 * (NVX - 1)) * SPACING
    ay = TIME_STEP * jnp.abs(vy)
    cy = 0.5 * ay * (1.0 - ay)
    forward = jnp.broadcast_to(vy > 0, (COLS, 128))
    sign = 2 * vt - 1
    offset = start + (1 - vt) * (count - 1)
    first = 2 + base + offset

    def chunk(m, carry):
        lanes = pl.ds(pl.multiple_of(m * 128, 128), 128)
        index = vt * HALF + m * 2 + lane // 64
        ax = TIME_STEP * jnp.abs((as_f32(index) - 0.5 * (NVX - 1)) * SPACING)
        cx = 0.5 * ax * (1.0 - ax)

        def row(px):
            return pad[px, TOP:TOP + COLS, lanes]

        u2, u1 = row(first - 2 * sign), row(first - sign)
        here = row(first)
        d0 = here - u1
        s1 = clamp_slope(u1 - u2, d0)
        for k in range(count):
            px = first + k * sign
            ahead = row(px + sign)
            dw = ahead - here
            s0 = clamp_slope(d0, dw)
            term_x = ax * d0 + cx * (s0 - s1)
            l1 = pad[px, TOP - 1:TOP - 1 + COLS, lanes]
            l2 = pad[px, TOP - 2:TOP - 2 + COLS, lanes]
            r1 = pad[px, TOP + 1:TOP + 1 + COLS, lanes]
            r2 = pad[px, TOP + 2:TOP + 2 + COLS, lanes]
            v1 = jnp.where(forward, l1, r1)
            v2 = jnp.where(forward, l2, r2)
            w1 = jnp.where(forward, r1, l1)
            e0 = here - v1
            t0 = clamp_slope(e0, w1 - here)
            t1 = clamp_slope(v1 - v2, e0)
            term_y = ay * e0 + cy * (t0 - t1)
            adv[offset + k * sign, :, lanes] = here - term_x - term_y
            here, d0, s1 = ahead, dw, s0
        return carry

    lax.fori_loop(0, LOCAL // 128, chunk, 0)


def wide(n):
    return pl.ds(pl.multiple_of(n * 256, 256), 256)


def stack(n, value, t_ref):
    hi, lo = split(value)
    t_ref[128 * n:128 * n + 128, :] = hi
    t_ref[1024 + 128 * n:1024 + 128 * n + 128, :] = lo


def to_parities(vt, adv, h_ref, t_ref, y_ref):
    cells = adv.reshape(CELLS, LOCAL)
    for n in range(8):
        stack(n, cells[:, wide(jnp.where(vt == 1, n, 7 - n))], t_ref)
    y = mm(t_ref[...], h_ref[0])
    for n in range(8):
        value = y[128 * n:128 * n + 128] + y[1024 + 128 * n:1024 + 128 * n + 128]
        for odd in range(2):
            y_ref[odd, :, 128 * n:128 * n + 128] = value[:, 128 * odd:128 * odd + 128]


def contract(vt, own, other, khi, klo, g_ref):
    sign = as_f32(1 - 2 * vt)
    for k in range(2):
        hi, lo = split(own[k] + sign * other[k])
        both = mm(jnp.concatenate([hi, lo], axis=0), khi[k])
        g_ref[k] = both[:CELLS] + both[CELLS:] + mm(hi, klo[k])


def from_parities(vt, own, other, h_ref, t_ref, adv, dens, kinds, inflow, put):
    sign = as_f32(2 * vt - 1)
    cells = adv.reshape(CELLS, LOCAL)
    for n in range(8):
        at = slice(128 * n, 128 * n + 128)
        stack(n, jnp.concatenate([own[k, :, at] + sign * other[k, :, at] for k in range(2)], axis=1), t_ref)
    back = mm(t_ref[...], h_ref[1])
    lane = iota((1, 256), 1)
    vy = (as_f32(lane % 64) - 0.5 * (NVX - 1)) * SPACING
    rate, kind = (jnp.concatenate([ref[...]] * 2, axis=1) for ref in (dens, kinds))
    for n in range(8):
        m = jnp.where(vt == 1, n, 7 - n)
        gain = (back[128 * n:128 * n + 128] + back[1024 + 128 * n:1024 + 128 * n + 128]) * GAIN_SCALE
        vx = (as_f32(vt * HALF + m * 4 + lane // 64) - 0.5 * (NVX - 1)) * SPACING
        nu = 1.0 + (vx * vx + vy * vy) / 8.0
        a = cells[:, wide(m)]
        after = a + rate * (gain - nu * a)
        after = jnp.where(kind == 1, 0.0, jnp.where(kind == 2, inflow[:, wide(m)], after))
        put(wide(m), after.reshape(GROUP, COLS, 256))


def kernel(dist, density, cell_type, inflow, out, pads, packs, halos, adv, yown, yin, gown, gin, t_ref,
           khi, klo, h_ref, dens_b, type_b, load_sem, xsend, xrecv, ysend, yrecv, fsend, frecv, qsend, qrecv):
    gx, gy, vt = lax.axis_index("gx"), lax.axis_index("gy"), lax.axis_index("vert")
    last = lax.axis_size("gy") - 1
    has_left, has_right = gy > 0, gy < last
    gets_two = gx == vt
    sides = ((0, has_left), (1, has_right))
    bases = ((1 - gx) * GROUP, gx * GROUP)

    load = pltpu.make_async_copy(dist, pads.at[0, pl.ds(2, ROWS), pl.ds(TOP, COLS), :], load_sem)
    load.start()

    barrier = pltpu.get_barrier_semaphore()
    pl.semaphore_signal(barrier, inc=1, device_id=(1 - gx, gy, vt), device_id_type=MESH)
    pl.semaphore_signal(barrier, inc=1, device_id=(gx, gy, 1 - vt), device_id_type=MESH)

    @pl.when(has_left)
    def _():
        pl.semaphore_signal(barrier, inc=1, device_id=(gx, gy - 1, vt), device_id_type=MESH)

    @pl.when(has_right)
    def _():
        pl.semaphore_signal(barrier, inc=1, device_id=(gx, gy + 1, vt), device_id_type=MESH)

    def x_copy(step, count):
        if count == 2:
            start, to = (1 - gx) * (ROWS - 2), gx * (ROWS + 2)
        else:
            start, to = (1 - gx) * (ROWS - 1), 1 + gx * (ROWS + 1)
        return pltpu.make_async_remote_copy(
            src_ref=pads.at[step, pl.ds(2 + start, count), pl.ds(TOP, COLS), :],
            dst_ref=pads.at[step, pl.ds(to, count), pl.ds(TOP, COLS), :],
            send_sem=xsend.at[step], recv_sem=xrecv.at[step],
            device_id=(1 - gx, gy, vt), device_id_type=MESH)

    def x_wait(step, count):
        if count == 2:
            to = (1 - gx) * (ROWS + 2)
        else:
            to = 1 + (1 - gx) * (ROWS + 1)
        return pltpu.make_async_remote_copy(
            src_ref=pads.at[step, pl.ds(to, count), pl.ds(TOP, COLS), :],
            dst_ref=pads.at[step, pl.ds(to, count), pl.ds(TOP, COLS), :],
            send_sem=xsend.at[step], recv_sem=xrecv.at[step],
            device_id=(1 - gx, gy, vt), device_id_type=MESH)

    def y_copy(step, group, side, to):
        return pltpu.make_async_remote_copy(
            src_ref=packs.at[step, group, side], dst_ref=halos.at[step, group, to],
            send_sem=ysend.at[step, group, side], recv_sem=yrecv.at[step, group, to],
            device_id=(gx, gy - 1 + 2 * side, vt), device_id_type=MESH)

    def send_x(step):
        pl.when(gets_two)(lambda: x_copy(step, 1).start())
        pl.when(jnp.logical_not(gets_two))(lambda: x_copy(step, 2).start())

    def send_y(step, group):
        for side, present in sides:
            y = TOP + side * (COLS - 2)
            for x in range(GROUP):
                at = 2 * (x % 4)
                packs[step, group, side, x // 4, at:at + 2, :] = pads[step, 2 + bases[group] + x, y:y + 2, :]
            pl.when(present)(lambda side=side: y_copy(step, group, side, 1 - side).start())

    def clear_missing(step):
        zero_row = jnp.zeros((COLS, LOCAL), F32)

        @pl.when(gets_two)
        def _():
            pads[step, 1 + vt * (ROWS + 1), pl.ds(TOP, COLS), :] = zero_row

        @pl.when(jnp.logical_not(gets_two))
        def _():
            for k in range(2):
                pads[step, (1 - vt) * (ROWS + 2) + k, pl.ds(TOP, COLS), :] = zero_row

        for side, present in sides:
            @pl.when(jnp.logical_not(present))
            def _():
                for group in range(2):
                    for part in range(2):
                        halos[step, group, side, part] = jnp.zeros((8, LOCAL), F32)

    def take_x(step):
        pl.when(gets_two)(lambda: x_wait(step, 2).wait_recv())
        pl.when(jnp.logical_not(gets_two))(lambda: x_wait(step, 1).wait_recv())

    def take_y(step, group):
        for side, present in sides:
            pl.when(present)(lambda side=side: y_copy(step, group, side, side).wait_recv())
            y = TOP - 2 + side * (COLS + 2)
            for x in range(GROUP):
                at = 2 * (x % 4)
                pads[step, 2 + bases[group] + x, y:y + 2, :] = halos[step, group, side, x // 4, at:at + 2, :]

    def wait_sent(step):
        pl.when(gets_two)(lambda: x_copy(step, 1).wait_send())
        pl.when(jnp.logical_not(gets_two))(lambda: x_copy(step, 2).wait_send())
        for group in range(2):
            for side, present in sides:
                pl.when(present)(lambda side=side, group=group: y_copy(step, group, side, side).wait_send())

    def partner_copy(src, dst, send, recv, step, group):
        return pltpu.make_async_remote_copy(
            src_ref=src.at[step, group], dst_ref=dst.at[step, group],
            send_sem=send.at[step, group], recv_sem=recv.at[step, group],
            device_id=(gx, gy, 1 - vt), device_id_type=MESH)

    def there(step, group):
        return partner_copy(yown, yin, fsend, frecv, step, group)

    def back(step, group):
        return partner_copy(gown, gin, qsend, qrecv, step, group)

    def stage_a(step, group, start=0, count=GROUP):
        advect(vt, pads.at[step], bases[group], start, count, adv.at[group])

    def stage_a_inner(step):
        stage_a(step, 0, 2 * gx, GROUP - 2)

    def stage_a_edge(step):
        stage_a(step, 0, (1 - gx) * (GROUP - 2), 2)

    def stage_t(step, group):
        to_parities(vt, adv.at[group], h_ref, t_ref, yown.at[step, group])
        there(step, group).start()

    def stage_c(step, group):
        there(step, group).wait_recv()
        contract(vt, yown.at[step, group], yin.at[step, group], khi, klo, gown.at[step, group])
        back(step, group).start()

    def stage_f(step, group):
        back(step, group).wait_recv()
        base = bases[group]
        if step < STEPS - 1:
            def put(lanes, value):
                pads[step + 1, pl.ds(2 + base, GROUP), TOP:TOP + COLS, lanes] = value
        else:
            def put(lanes, value):
                out[pl.ds(base, GROUP), :, lanes] = value
        cells = pl.ds(pl.multiple_of(base * COLS, CELLS), CELLS)
        from_parities(vt, gown.at[step, group], gin.at[step, group], h_ref, t_ref, adv.at[group],
                      dens_b.at[cells], type_b.at[cells], inflow, put)

    load.wait()
    pl.semaphore_wait(barrier, 2 + has_left.astype(jnp.int32) + has_right.astype(jnp.int32))
    send_x(0)
    for group in range(2):
        send_y(0, group)
    for step in range(STEPS):
        clear_missing(step)
    rate = (COLLISION_RATE * density[...]).T
    kind = as_f32(cell_type[...]).T
    for x in range(ROWS):
        dens_b[x * COLS:x * COLS + COLS] = jnp.broadcast_to(rate[:, x:x + 1], (COLS, 128))
        type_b[x * COLS:x * COLS + COLS] = jnp.broadcast_to(kind[:, x:x + 1], (COLS, 128))
    parity_maps(vt, h_ref)
    make_kernel_blocks(vt, khi, klo)

    for step in range(STEPS):
        take_y(step, 1)
        stage_a(step, 1)
        stage_t(step, 1)
        take_y(step, 0)
        stage_a_inner(step)
        stage_c(step, 1)
        take_x(step)
        stage_a_edge(step)
        stage_t(step, 0)
        stage_f(step, 1)
        if step < STEPS - 1:
            send_y(step + 1, 1)
        stage_c(step, 0)
        stage_f(step, 0)
        if step < STEPS - 1:
            send_x(step + 1)
            send_y(step + 1, 0)
    for step in range(STEPS):
        wait_sent(step)
        for group in range(2):
            there(step, group).wait_send()
            back(step, group).wait_send()


def per_device(distribution, density, cell_type, inflow):
    vmem = pl.BlockSpec(memory_space=pltpu.VMEM)
    dma = pltpu.SemaphoreType.DMA
    pair = pltpu.VMEM((STEPS, 2, 2, CELLS, 1024), F32)
    return pl.pallas_call(
        kernel,
        out_shape=jax.ShapeDtypeStruct((ROWS, COLS, LOCAL), F32),
        in_specs=[pl.BlockSpec(memory_space=pl.ANY), vmem, vmem, vmem],
        out_specs=vmem,
        scratch_shapes=[
            pltpu.VMEM((STEPS, PAD_X, PAD_Y, LOCAL), F32),
            pltpu.VMEM((STEPS, 2, 2, 2, 8, LOCAL), F32),
            pltpu.VMEM((STEPS, 2, 2, 2, 8, LOCAL), F32),
            pltpu.VMEM((2, GROUP, COLS, LOCAL), F32),
            pair, pair, pair, pair,
            pltpu.VMEM((2048, 256), BF16),
            pltpu.VMEM((2, 1024, 1024), BF16),
            pltpu.VMEM((2, 1024, 1024), BF16),
            pltpu.VMEM((2, 256, 256), BF16),
            pltpu.VMEM((ROWS * COLS, 128), F32),
            pltpu.VMEM((ROWS * COLS, 128), F32),
            dma,
            dma((STEPS,)), dma((STEPS,)),
            dma((STEPS, 2, 2)), dma((STEPS, 2, 2)),
            dma((STEPS, 2)), dma((STEPS, 2)),
            dma((STEPS, 2)), dma((STEPS, 2)),
        ],
        compiler_params=pltpu.CompilerParams(
            collective_id=0, has_side_effects=True, vmem_limit_bytes=67000000),
    )(distribution, density, cell_type, inflow.reshape(1, LOCAL))


def solution(mesh):
    placed = (P("gx", "gy", "vert"), P("gx", "gy"), P("gx", "gy"), P("vert"))
    return jax.shard_map(
        per_device, mesh=mesh, in_specs=placed, out_specs=P("gx", "gy", "vert"), check_vma=False
    )
```

```python
import functools

import jax
import jax.numpy as jnp
from jax import lax
from jax.experimental import pallas as pl
from jax.experimental.pallas import tpu as pltpu
from jax.sharding import PartitionSpec as P

MESH = pl.DeviceIdType.MESH
F32 = jnp.float32
BF16 = jnp.bfloat16

NVX = 64
HALF = 32
STEPS = 2
SPACING = 8.0 / NVX
TIME_STEP = 0.1
COLLISION_RATE = 0.2
GAIN_SCALE = 2.0 * 2.5 * SPACING * SPACING / 4.0
LOG2E = 1.4426950408889634

ROWS = 16
COLS = 16
GROUP = 8
CELLS = GROUP * COLS
LOCAL = 2048
PAD_X = ROWS + 4
PAD_Y = 32
TOP = 8


def iota(shape, dim):
    return lax.broadcasted_iota(jnp.int32, shape, dim)


def as_f32(x):
    return x.astype(F32)


def clamp_slope(a, b):
    return jnp.minimum(jnp.maximum(b, jnp.minimum(a, 0.0)), jnp.maximum(a, 0.0))


def split(x):
    hi = x.astype(BF16)
    lo = (x - hi.astype(F32)).astype(BF16)
    return hi, lo


def mm(a, b):
    return jnp.dot(a, b, preferred_element_type=F32)


def parity_maps(vt, h_ref):
    row, col = iota((256, 256), 0), iota((256, 256), 1)
    for k, (lane, out) in enumerate(((row, col), (col, row))):
        odd, out_i, b = out // 128, (out // 32) % 4, out % 32
        lane_i, j = lane // 64, lane % 64
        same = lane_i == jnp.where(vt == 1, out_i, 3 - out_i)
        upper = (j == HALF + b) & same
        lower = (j == HALF - 1 - b) & same
        value = jnp.where(upper, 1.0, jnp.where(lower, jnp.where(odd == 1, -1.0, 1.0), 0.0))
        h_ref[k] = value.astype(BF16)


def magnitude(i):
    return (as_f32(i) + 0.5) * SPACING


def make_kernel_blocks(vt, khi, klo):
    qv = (as_f32(iota((32, 128), 1) % 32) + 0.5) * SPACING
    qw = (as_f32(iota((32, 128), 0)) + 0.5) * SPACING
    dy = ((qv - qw) * (qv - qw) + SPACING * SPACING, (qv + qw) * (qv + qw) + SPACING * SPACING)
    ey = qv * qv - qw * qw
    gy = jnp.exp(-(qv * qv + qw * qw) / 4.0) * 0.5
    lane_i = iota((1, 128), 1) // 32
    sign = as_f32(1 - 2 * vt)

    def tile(t, carry):
        n, i = t // 32, t % 32
        pv = magnitude(n * 4 + lane_i)
        pw = magnitude(jnp.zeros((1, 128), jnp.int32) + i)
        e = ey + (pv * pv - pw * pw)
        e2 = e * e
        g = gy * jnp.exp(-(pv * pv + pw * pw) / 4.0)
        dx = ((pv - pw) * (pv - pw), (pv + pw) * (pv + pw))
        parts = []
        for a in range(2):
            for b in range(2):
                r2 = dy[b] + dx[a]
                rs = lax.rsqrt(r2)
                arg = (r2 + e2 * (rs * rs)) * (-LOG2E / 8.0)
                parts.append(jnp.exp2(arg) * rs - (r2 * rs) * g)
        mm_, mp, pm, pp = parts
        sm, dm = mm_ + mp, mm_ - mp
        sp, dp = pm + pp, pm - pp
        blocks = (sm + sign * sp, dm + sign * dp)
        at = pl.ds(pl.multiple_of(i * 32, 32), 32)
        lanes = pl.ds(pl.multiple_of(n * 128, 128), 128)
        for k in range(2):
            hi, lo = split(blocks[k])
            khi[k, at, lanes] = hi
            klo[k, at, lanes] = lo
        return carry

    lax.fori_loop(0, 256, tile, 0)


def advect(vt, pad, base, start, count, adv):
    lane = iota((1, 128), 1)
    vy = (as_f32(lane % 64) - 0.5 * (NVX - 1)) * SPACING
    ay = TIME_STEP * jnp.abs(vy)
    cy = 0.5 * ay * (1.0 - ay)
    forward = jnp.broadcast_to(vy > 0, (COLS, 128))
    sign = 2 * vt - 1
    offset = start + (1 - vt) * (count - 1)
    first = 2 + base + offset

    def chunk(m, carry):
        lanes = pl.ds(pl.multiple_of(m * 128, 128), 128)
        index = vt * HALF + m * 2 + lane // 64
        ax = TIME_STEP * jnp.abs((as_f32(index) - 0.5 * (NVX - 1)) * SPACING)
        cx = 0.5 * ax * (1.0 - ax)

        def row(px):
            return pad[px, TOP:TOP + COLS, lanes]

        u2, u1 = row(first - 2 * sign), row(first - sign)
        here = row(first)
        d0 = here - u1
        s1 = clamp_slope(u1 - u2, d0)
        for k in range(count):
            px = first + k * sign
            ahead = row(px + sign)
            dw = ahead - here
            s0 = clamp_slope(d0, dw)
            term_x = ax * d0 + cx * (s0 - s1)
            l1 = pad[px, TOP - 1:TOP - 1 + COLS, lanes]
            l2 = pad[px, TOP - 2:TOP - 2 + COLS, lanes]
            r1 = pad[px, TOP + 1:TOP + 1 + COLS, lanes]
            r2 = pad[px, TOP + 2:TOP + 2 + COLS, lanes]
            v1 = jnp.where(forward, l1, r1)
            v2 = jnp.where(forward, l2, r2)
            w1 = jnp.where(forward, r1, l1)
            e0 = here - v1
            t0 = clamp_slope(e0, w1 - here)
            t1 = clamp_slope(v1 - v2, e0)
            term_y = ay * e0 + cy * (t0 - t1)
            adv[offset + k * sign, :, lanes] = here - term_x - term_y
            here, d0, s1 = ahead, dw, s0
        return carry

    lax.fori_loop(0, LOCAL // 128, chunk, 0)


def wide(n):
    return pl.ds(pl.multiple_of(n * 256, 256), 256)


def stack(n, count, value, t_ref):
    hi, lo = split(value)
    t_ref[count * n:count * n + count, :] = hi
    t_ref[count * (8 + n):count * (8 + n) + count, :] = lo


def joined(n, count, value):
    return value[count * n:count * n + count] + value[count * (8 + n):count * (8 + n) + count]


def cell_range(row, rows):
    return pl.ds(pl.multiple_of(row * COLS, 2 * COLS), rows * COLS)


def to_parities(vt, adv, row, rows, h_ref, t_ref, y_ref):
    cells, count, at = adv.reshape(CELLS, LOCAL), rows * COLS, cell_range(row, rows)
    for n in range(8):
        stack(n, count, cells[at, wide(jnp.where(vt == 1, n, 7 - n))], t_ref)
    y = mm(t_ref[:16 * count], h_ref[0])
    for n in range(8):
        value = joined(n, count, y)
        for odd in range(2):
            y_ref[odd, at, 128 * n:128 * n + 128] = value[:, 128 * odd:128 * odd + 128]


def contract(vt, own, other, khi, klo, g_ref, send):
    sign = as_f32(1 - 2 * vt)
    for k in range(2):
        hi, lo = split(own[k] + sign * other[k])
        both = mm(jnp.concatenate([hi, lo], axis=0), khi[k])
        g_ref[k] = both[:CELLS] + both[CELLS:] + mm(hi, klo[k])
        send(k)


def from_parities(vt, own, other, row, rows, h_ref, t_ref, adv, dens, kinds, inflow, put):
    sign = as_f32(2 * vt - 1)
    cells, count, at = adv.reshape(CELLS, LOCAL), rows * COLS, cell_range(row, rows)
    for n in range(8):
        lanes = slice(128 * n, 128 * n + 128)
        both = [own[k, at, lanes] + sign * other[k, at, lanes] for k in range(2)]
        stack(n, count, jnp.concatenate(both, axis=1), t_ref)
    back = mm(t_ref[:16 * count], h_ref[1])
    lane = iota((1, 256), 1)
    vy = (as_f32(lane % 64) - 0.5 * (NVX - 1)) * SPACING
    rate, kind = (jnp.concatenate([ref[at, :]] * 2, axis=1) for ref in (dens, kinds))
    for n in range(8):
        m = jnp.where(vt == 1, n, 7 - n)
        gain = joined(n, count, back) * GAIN_SCALE
        vx = (as_f32(vt * HALF + m * 4 + lane // 64) - 0.5 * (NVX - 1)) * SPACING
        nu = 1.0 + (vx * vx + vy * vy) / 8.0
        a = cells[at, wide(m)]
        after = a + rate * (gain - nu * a)
        after = jnp.where(kind == 1, 0.0, jnp.where(kind == 2, inflow[:, wide(m)], after))
        put(wide(m), after.reshape(rows, COLS, 256))


def kernel(dist, density, cell_type, inflow, result, pads, packs, halos, adv, yown, yin, gown, gin, t_ref,
           khi, klo, h_ref, dens_b, type_b, out, load_sem, store_sem, xsend, xrecv, ysend, yrecv, fsend, frecv, qsend, qrecv):
    gx, gy, vt = lax.axis_index("gx"), lax.axis_index("gy"), lax.axis_index("vert")
    last = lax.axis_size("gy") - 1
    has_left, has_right = gy > 0, gy < last
    gets_two = gx == vt
    sides = ((0, has_left), (1, has_right))
    bases = ((1 - gx) * GROUP, gx * GROUP)

    load = pltpu.make_async_copy(dist, pads.at[0, pl.ds(2, ROWS), pl.ds(TOP, COLS), :], load_sem)
    load.start()

    barrier = pltpu.get_barrier_semaphore()
    pl.semaphore_signal(barrier, inc=1, device_id=(1 - gx, gy, vt), device_id_type=MESH)
    pl.semaphore_signal(barrier, inc=1, device_id=(gx, gy, 1 - vt), device_id_type=MESH)

    @pl.when(has_left)
    def _():
        pl.semaphore_signal(barrier, inc=1, device_id=(gx, gy - 1, vt), device_id_type=MESH)

    @pl.when(has_right)
    def _():
        pl.semaphore_signal(barrier, inc=1, device_id=(gx, gy + 1, vt), device_id_type=MESH)

    def x_copy(step, count):
        if count == 2:
            start, to = (1 - gx) * (ROWS - 2), gx * (ROWS + 2)
        else:
            start, to = (1 - gx) * (ROWS - 1), 1 + gx * (ROWS + 1)
        return pltpu.make_async_remote_copy(
            src_ref=pads.at[step, pl.ds(2 + start, count), pl.ds(TOP, COLS), :],
            dst_ref=pads.at[step, pl.ds(to, count), pl.ds(TOP, COLS), :],
            send_sem=xsend.at[step], recv_sem=xrecv.at[step],
            device_id=(1 - gx, gy, vt), device_id_type=MESH)

    def x_wait(step, count):
        if count == 2:
            to = (1 - gx) * (ROWS + 2)
        else:
            to = 1 + (1 - gx) * (ROWS + 1)
        return pltpu.make_async_remote_copy(
            src_ref=pads.at[step, pl.ds(to, count), pl.ds(TOP, COLS), :],
            dst_ref=pads.at[step, pl.ds(to, count), pl.ds(TOP, COLS), :],
            send_sem=xsend.at[step], recv_sem=xrecv.at[step],
            device_id=(1 - gx, gy, vt), device_id_type=MESH)

    def y_copy(step, group, side, to):
        return pltpu.make_async_remote_copy(
            src_ref=packs.at[step, group, side], dst_ref=halos.at[step, group, to],
            send_sem=ysend.at[step, group, side], recv_sem=yrecv.at[step, group, to],
            device_id=(gx, gy - 1 + 2 * side, vt), device_id_type=MESH)

    def send_x(step):
        pl.when(gets_two)(lambda: x_copy(step, 1).start())
        pl.when(jnp.logical_not(gets_two))(lambda: x_copy(step, 2).start())

    def send_y(step, group):
        for side, present in sides:
            y = TOP + side * (COLS - 2)
            for x in range(GROUP):
                at = 2 * (x % 4)
                packs[step, group, side, x // 4, at:at + 2, :] = pads[step, 2 + bases[group] + x, y:y + 2, :]
            pl.when(present)(lambda side=side: y_copy(step, group, side, 1 - side).start())

    def clear_missing(step):
        zero_row = jnp.zeros((COLS, LOCAL), F32)

        @pl.when(gets_two)
        def _():
            pads[step, 1 + vt * (ROWS + 1), pl.ds(TOP, COLS), :] = zero_row

        @pl.when(jnp.logical_not(gets_two))
        def _():
            for k in range(2):
                pads[step, (1 - vt) * (ROWS + 2) + k, pl.ds(TOP, COLS), :] = zero_row

        for side, present in sides:
            @pl.when(jnp.logical_not(present))
            def _():
                for group in range(2):
                    for part in range(2):
                        halos[step, group, side, part] = jnp.zeros((8, LOCAL), F32)

    def take_x(step):
        pl.when(gets_two)(lambda: x_wait(step, 2).wait_recv())
        pl.when(jnp.logical_not(gets_two))(lambda: x_wait(step, 1).wait_recv())

    def take_y(step, group):
        for side, present in sides:
            pl.when(present)(lambda side=side: y_copy(step, group, side, side).wait_recv())
            y = TOP - 2 + side * (COLS + 2)
            for x in range(GROUP):
                at = 2 * (x % 4)
                pads[step, 2 + bases[group] + x, y:y + 2, :] = halos[step, group, side, x // 4, at:at + 2, :]

    def wait_sent(step):
        pl.when(gets_two)(lambda: x_copy(step, 1).wait_send())
        pl.when(jnp.logical_not(gets_two))(lambda: x_copy(step, 2).wait_send())
        for group in range(2):
            for side, present in sides:
                pl.when(present)(lambda side=side, group=group: y_copy(step, group, side, side).wait_send())

    parts = ((0, 2 * gx, GROUP - 2), (0, (1 - gx) * (GROUP - 2), 2), (1, 0, GROUP))

    def store(part):
        group, row, rows = parts[part]
        at = pl.ds(bases[group] + row, rows)
        return pltpu.make_async_copy(out.at[at], result.at[at], store_sem.at[part])

    def there(step, part):
        group, row, rows = parts[part]
        at = cell_range(row, rows)
        return pltpu.make_async_remote_copy(
            src_ref=yown.at[step, group, :, at, :], dst_ref=yin.at[step, group, :, at, :],
            send_sem=fsend.at[step, part], recv_sem=frecv.at[step, part],
            device_id=(gx, gy, 1 - vt), device_id_type=MESH)

    def back(step, group, k):
        return pltpu.make_async_remote_copy(
            src_ref=gown.at[step, group, k], dst_ref=gin.at[step, group, k],
            send_sem=qsend.at[step, group, k], recv_sem=qrecv.at[step, group, k],
            device_id=(gx, gy, 1 - vt), device_id_type=MESH)

    def stage_a(step, part):
        group, row, rows = parts[part]
        advect(vt, pads.at[step], bases[group], row, rows, adv.at[group])

    def stage_t(step, part):
        group, row, rows = parts[part]
        to_parities(vt, adv.at[group], row, rows, h_ref, t_ref, yown.at[step, group])
        there(step, part).start()

    def stage_c(step, group):
        for part in ((0, 1), (2,))[group]:
            there(step, part).wait_recv()
        contract(vt, yown.at[step, group], yin.at[step, group], khi, klo, gown.at[step, group],
                 lambda k: back(step, group, k).start())

    def stage_f(step, part):
        group, row, rows = parts[part]
        base = bases[group]
        if step < STEPS - 1:
            def put(lanes, value):
                pads[step + 1, pl.ds(2 + base + row, rows), TOP:TOP + COLS, lanes] = value
        else:
            def put(lanes, value):
                out[pl.ds(base + row, rows), :, lanes] = value
        cells = pl.ds(pl.multiple_of(base * COLS, CELLS), CELLS)
        from_parities(vt, gown.at[step, group], gin.at[step, group], row, rows, h_ref, t_ref, adv.at[group],
                      dens_b.at[cells], type_b.at[cells], inflow, put)

        if step == STEPS - 1:
            store(part).start()

    def take_gains(step, group):
        for k in range(2):
            back(step, group, k).wait_recv()

    load.wait()
    pl.semaphore_wait(barrier, 2 + has_left.astype(jnp.int32) + has_right.astype(jnp.int32))
    send_x(0)
    for group in range(2):
        send_y(0, group)
    for step in range(STEPS):
        clear_missing(step)
    rate = (COLLISION_RATE * density[...]).T
    kind = as_f32(cell_type[...]).T
    for x in range(ROWS):
        dens_b[x * COLS:x * COLS + COLS] = jnp.broadcast_to(rate[:, x:x + 1], (COLS, 128))
        type_b[x * COLS:x * COLS + COLS] = jnp.broadcast_to(kind[:, x:x + 1], (COLS, 128))
    parity_maps(vt, h_ref)
    make_kernel_blocks(vt, khi, klo)

    for step in range(STEPS):
        final = step == STEPS - 1
        take_y(step, 1)
        stage_a(step, 2)
        stage_t(step, 2)
        take_y(step, 0)
        stage_a(step, 0)
        stage_t(step, 0)
        stage_c(step, 1)
        take_x(step)
        stage_a(step, 1)
        stage_t(step, 1)
        take_gains(step, 1)
        stage_f(step, 2)
        if not final:
            send_y(step + 1, 1)
        stage_c(step, 0)
        take_gains(step, 0)
        stage_f(step, 1)
        if not final:
            send_x(step + 1)
        stage_f(step, 0)
        if not final:
            send_y(step + 1, 0)
    for part in range(3):
        store(part).wait()
    for step in range(STEPS):
        wait_sent(step)
        for part in range(3):
            there(step, part).wait_send()
        for group in range(2):
            for k in range(2):
                back(step, group, k).wait_send()


def per_device(distribution, density, cell_type, inflow):
    vmem = pl.BlockSpec(memory_space=pltpu.VMEM)
    dma = pltpu.SemaphoreType.DMA
    pair = pltpu.VMEM((STEPS, 2, 2, CELLS, 1024), F32)
    return pl.pallas_call(
        kernel,
        out_shape=jax.ShapeDtypeStruct((ROWS, COLS, LOCAL), F32),
        in_specs=[pl.BlockSpec(memory_space=pl.ANY), vmem, vmem, vmem],
        out_specs=pl.BlockSpec(memory_space=pl.ANY),
        scratch_shapes=[
            pltpu.VMEM((STEPS, PAD_X, PAD_Y, LOCAL), F32),
            pltpu.VMEM((STEPS, 2, 2, 2, 8, LOCAL), F32),
            pltpu.VMEM((STEPS, 2, 2, 2, 8, LOCAL), F32),
            pltpu.VMEM((2, GROUP, COLS, LOCAL), F32),
            pair, pair, pair, pair,
            pltpu.VMEM((2048, 256), BF16),
            pltpu.VMEM((2, 1024, 1024), BF16),
            pltpu.VMEM((2, 1024, 1024), BF16),
            pltpu.VMEM((2, 256, 256), BF16),
            pltpu.VMEM((ROWS * COLS, 128), F32),
            pltpu.VMEM((ROWS * COLS, 128), F32),
            pltpu.VMEM((ROWS, COLS, LOCAL), F32),
            dma, dma((3,)),
            dma((STEPS,)), dma((STEPS,)),
            dma((STEPS, 2, 2)), dma((STEPS, 2, 2)),
            dma((STEPS, 3)), dma((STEPS, 3)),
            dma((STEPS, 2, 2)), dma((STEPS, 2, 2)),
        ],
        compiler_params=pltpu.CompilerParams(
            collective_id=0, has_side_effects=True, vmem_limit_bytes=46 << 20),
    )(distribution, density, cell_type, inflow.reshape(1, LOCAL))


def solution(mesh):
    placed = (P("gx", "gy", "vert"), P("gx", "gy"), P("gx", "gy"), P("vert"))
    return jax.shard_map(
        per_device, mesh=mesh, in_specs=placed, out_specs=P("gx", "gy", "vert"), check_vma=False
    )
```

```python
import functools

import jax
import jax.numpy as jnp
from jax import lax
from jax.experimental import pallas as pl
from jax.experimental.pallas import tpu as pltpu
from jax.sharding import PartitionSpec as P

MESH = pl.DeviceIdType.MESH
F32 = jnp.float32
BF16 = jnp.bfloat16

NVX = 64
HALF = 32
STEPS = 2
SPACING = 8.0 / NVX
TIME_STEP = 0.1
COLLISION_RATE = 0.2
GAIN_SCALE = 2.0 * 2.5 * SPACING * SPACING / 4.0
LOG2E = 1.4426950408889634

ROWS = 16
COLS = 16
GROUP = 8
CELLS = GROUP * COLS
LOCAL = 2048
PAD_X = ROWS + 4
PAD_Y = 32
TOP = 8


def iota(shape, dim):
    return lax.broadcasted_iota(jnp.int32, shape, dim)


def as_f32(x):
    return x.astype(F32)


def clamp_slope(a, b):
    return jnp.minimum(jnp.maximum(b, jnp.minimum(a, 0.0)), jnp.maximum(a, 0.0))


def split(x):
    hi = x.astype(BF16)
    lo = (x - hi.astype(F32)).astype(BF16)
    return hi, lo


def mm(a, b):
    return jnp.dot(a, b, preferred_element_type=F32)


def parity_maps(vt, h_ref):
    row, col = iota((256, 256), 0), iota((256, 256), 1)
    for k, (lane, out) in enumerate(((row, col), (col, row))):
        odd, out_i, b = out // 128, (out // 32) % 4, out % 32
        lane_i, j = lane // 64, lane % 64
        same = lane_i == jnp.where(vt == 1, out_i, 3 - out_i)
        upper = (j == HALF + b) & same
        lower = (j == HALF - 1 - b) & same
        value = jnp.where(upper, 1.0, jnp.where(lower, jnp.where(odd == 1, -1.0, 1.0), 0.0))
        h_ref[k] = value.astype(BF16)


def magnitude(i):
    return (as_f32(i) + 0.5) * SPACING


def make_kernel_blocks(vt, khi, klo):
    qv = (as_f32(iota((32, 128), 1) % 32) + 0.5) * SPACING
    qw = (as_f32(iota((32, 128), 0)) + 0.5) * SPACING
    dy = ((qv - qw) * (qv - qw) + SPACING * SPACING, (qv + qw) * (qv + qw) + SPACING * SPACING)
    ey = qv * qv - qw * qw
    gy = jnp.exp(-(qv * qv + qw * qw) / 4.0) * 0.5
    lane_i = iota((1, 128), 1) // 32
    sign = as_f32(1 - 2 * vt)

    def tile(t, carry):
        n, i = t // 32, t % 32
        pv = magnitude(n * 4 + lane_i)
        pw = magnitude(jnp.zeros((1, 128), jnp.int32) + i)
        e = ey + (pv * pv - pw * pw)
        e2 = e * e
        g = gy * jnp.exp(-(pv * pv + pw * pw) / 4.0)
        dx = ((pv - pw) * (pv - pw), (pv + pw) * (pv + pw))
        parts = []
        for a in range(2):
            for b in range(2):
                r2 = dy[b] + dx[a]
                rs = lax.rsqrt(r2)
                arg = (r2 + e2 * (rs * rs)) * (-LOG2E / 8.0)
                parts.append(jnp.exp2(arg) * rs - (r2 * rs) * g)
        mm_, mp, pm, pp = parts
        sm, dm = mm_ + mp, mm_ - mp
        sp, dp = pm + pp, pm - pp
        blocks = (sm + sign * sp, dm + sign * dp)
        at = pl.ds(pl.multiple_of(i * 32, 32), 32)
        lanes = pl.ds(pl.multiple_of(n * 128, 128), 128)
        for k in range(2):
            hi, lo = split(blocks[k])
            khi[k, at, lanes] = hi
            klo[k, at, lanes] = lo
        return carry

    lax.fori_loop(0, 256, tile, 0)


def advect(vt, pad, base, start, count, adv):
    lane = iota((1, 128), 1)
    vy = (as_f32(lane % 64) - 0.5 * (NVX - 1)) * SPACING
    ay = TIME_STEP * jnp.abs(vy)
    cy = 0.5 * ay * (1.0 - ay)
    forward = jnp.broadcast_to(vy > 0, (COLS, 128))
    sign = 2 * vt - 1
    offset = start + (1 - vt) * (count - 1)
    first = 2 + base + offset

    def chunk(m, carry):
        lanes = pl.ds(pl.multiple_of(m * 128, 128), 128)
        index = vt * HALF + m * 2 + lane // 64
        ax = TIME_STEP * jnp.abs((as_f32(index) - 0.5 * (NVX - 1)) * SPACING)
        cx = 0.5 * ax * (1.0 - ax)

        def row(px):
            return pad[px, TOP:TOP + COLS, lanes]

        u2, u1 = row(first - 2 * sign), row(first - sign)
        here = row(first)
        d0 = here - u1
        s1 = clamp_slope(u1 - u2, d0)
        for k in range(count):
            px = first + k * sign
            ahead = row(px + sign)
            dw = ahead - here
            s0 = clamp_slope(d0, dw)
            term_x = ax * d0 + cx * (s0 - s1)
            l1 = pad[px, TOP - 1:TOP - 1 + COLS, lanes]
            l2 = pad[px, TOP - 2:TOP - 2 + COLS, lanes]
            r1 = pad[px, TOP + 1:TOP + 1 + COLS, lanes]
            r2 = pad[px, TOP + 2:TOP + 2 + COLS, lanes]
            v1 = jnp.where(forward, l1, r1)
            v2 = jnp.where(forward, l2, r2)
            w1 = jnp.where(forward, r1, l1)
            e0 = here - v1
            t0 = clamp_slope(e0, w1 - here)
            t1 = clamp_slope(v1 - v2, e0)
            term_y = ay * e0 + cy * (t0 - t1)
            adv[offset + k * sign, :, lanes] = here - term_x - term_y
            here, d0, s1 = ahead, dw, s0
        return carry

    lax.fori_loop(0, LOCAL // 128, chunk, 0)


def wide(n):
    return pl.ds(pl.multiple_of(n * 256, 256), 256)


def stack(n, count, value, t_ref):
    hi, lo = split(value)
    t_ref[count * n:count * n + count, :] = hi
    t_ref[count * (8 + n):count * (8 + n) + count, :] = lo


def joined(n, count, value):
    return value[count * n:count * n + count] + value[count * (8 + n):count * (8 + n) + count]


def cell_range(row, rows):
    return pl.ds(pl.multiple_of(row * COLS, 2 * COLS), rows * COLS)


def to_parities(vt, adv, row, rows, h_ref, t_ref, y_ref):
    cells, count, at = adv.reshape(CELLS, LOCAL), rows * COLS, cell_range(row, rows)
    for n in range(8):
        stack(n, count, cells[at, wide(jnp.where(vt == 1, n, 7 - n))], t_ref)
    y = mm(t_ref[:16 * count], h_ref[0])
    for n in range(8):
        value = joined(n, count, y)
        for odd in range(2):
            y_ref[odd, at, 128 * n:128 * n + 128] = value[:, 128 * odd:128 * odd + 128]


def contract(vt, own, other, khi, klo, g_ref, send):
    sign = as_f32(1 - 2 * vt)
    for k in range(2):
        hi, lo = split(own[k] + sign * other[k])
        both = mm(jnp.concatenate([hi, lo], axis=0), khi[k])
        g_ref[k] = both[:CELLS] + both[CELLS:] + mm(hi, klo[k])
        send(k)


def from_parities(vt, own, other, row, rows, h_ref, t_ref, adv, dens, kinds, inflow, put):
    sign = as_f32(2 * vt - 1)
    cells, count, at = adv.reshape(CELLS, LOCAL), rows * COLS, cell_range(row, rows)
    for n in range(8):
        lanes = slice(128 * n, 128 * n + 128)
        both = [own[k, at, lanes] + sign * other[k, at, lanes] for k in range(2)]
        stack(n, count, jnp.concatenate(both, axis=1), t_ref)
    back = mm(t_ref[:16 * count], h_ref[1])
    lane = iota((1, 256), 1)
    vy = (as_f32(lane % 64) - 0.5 * (NVX - 1)) * SPACING
    rate, kind = (jnp.concatenate([ref[at, :]] * 2, axis=1) for ref in (dens, kinds))
    for n in range(8):
        m = jnp.where(vt == 1, n, 7 - n)
        gain = joined(n, count, back) * GAIN_SCALE
        vx = (as_f32(vt * HALF + m * 4 + lane // 64) - 0.5 * (NVX - 1)) * SPACING
        nu = 1.0 + (vx * vx + vy * vy) / 8.0
        a = cells[at, wide(m)]
        after = a + rate * (gain - nu * a)
        after = jnp.where(kind == 1, 0.0, jnp.where(kind == 2, inflow[:, wide(m)], after))
        put(wide(m), after.reshape(rows, COLS, 256))


def kernel(dist, density_in, cell_type_in, inflow_in, result, pads, packs, halos, adv, yown, yin, gown, gin, t_ref,
           khi, klo, h_ref, dens_b, type_b, out, density, cell_type, inflow, load_sem, store_sem, xsend, xrecv, ysend, yrecv, fsend, frecv, qsend, qrecv):
    gx, gy, vt = lax.axis_index("gx"), lax.axis_index("gy"), lax.axis_index("vert")
    last = lax.axis_size("gy") - 1
    has_left, has_right = gy > 0, gy < last
    gets_two = gx == vt
    sides = ((0, has_left), (1, has_right))
    bases = ((1 - gx) * GROUP, gx * GROUP)

    load = pltpu.make_async_copy(dist, pads.at[0, pl.ds(2, ROWS), pl.ds(TOP, COLS), :], load_sem.at[0])
    load.start()
    small = [pltpu.make_async_copy(src, dst, load_sem.at[1 + k]) for k, (src, dst) in enumerate(
        ((density_in, density), (cell_type_in, cell_type), (inflow_in, inflow)))]
    for copy in small:
        copy.start()

    barrier = pltpu.get_barrier_semaphore()
    pl.semaphore_signal(barrier, inc=1, device_id=(1 - gx, gy, vt), device_id_type=MESH)
    pl.semaphore_signal(barrier, inc=1, device_id=(gx, gy, 1 - vt), device_id_type=MESH)

    @pl.when(has_left)
    def _():
        pl.semaphore_signal(barrier, inc=1, device_id=(gx, gy - 1, vt), device_id_type=MESH)

    @pl.when(has_right)
    def _():
        pl.semaphore_signal(barrier, inc=1, device_id=(gx, gy + 1, vt), device_id_type=MESH)

    def x_copy(step, count):
        if count == 2:
            start, to = (1 - gx) * (ROWS - 2), gx * (ROWS + 2)
        else:
            start, to = (1 - gx) * (ROWS - 1), 1 + gx * (ROWS + 1)
        return pltpu.make_async_remote_copy(
            src_ref=pads.at[step, pl.ds(2 + start, count), pl.ds(TOP, COLS), :],
            dst_ref=pads.at[step, pl.ds(to, count), pl.ds(TOP, COLS), :],
            send_sem=xsend.at[step], recv_sem=xrecv.at[step],
            device_id=(1 - gx, gy, vt), device_id_type=MESH)

    def x_wait(step, count):
        if count == 2:
            to = (1 - gx) * (ROWS + 2)
        else:
            to = 1 + (1 - gx) * (ROWS + 1)
        return pltpu.make_async_remote_copy(
            src_ref=pads.at[step, pl.ds(to, count), pl.ds(TOP, COLS), :],
            dst_ref=pads.at[step, pl.ds(to, count), pl.ds(TOP, COLS), :],
            send_sem=xsend.at[step], recv_sem=xrecv.at[step],
            device_id=(1 - gx, gy, vt), device_id_type=MESH)

    def y_copy(step, group, side, to):
        return pltpu.make_async_remote_copy(
            src_ref=packs.at[step, group, side], dst_ref=halos.at[step, group, to],
            send_sem=ysend.at[step, group, side], recv_sem=yrecv.at[step, group, to],
            device_id=(gx, gy - 1 + 2 * side, vt), device_id_type=MESH)

    def send_x(step):
        pl.when(gets_two)(lambda: x_copy(step, 1).start())
        pl.when(jnp.logical_not(gets_two))(lambda: x_copy(step, 2).start())

    def send_y(step, group):
        for side, present in sides:
            y = TOP + side * (COLS - 2)
            for x in range(GROUP):
                at = 2 * (x % 4)
                packs[step, group, side, x // 4, at:at + 2, :] = pads[step, 2 + bases[group] + x, y:y + 2, :]
            pl.when(present)(lambda side=side: y_copy(step, group, side, 1 - side).start())

    def clear_missing(step):
        zero_row = jnp.zeros((COLS, LOCAL), F32)

        @pl.when(gets_two)
        def _():
            pads[step, 1 + vt * (ROWS + 1), pl.ds(TOP, COLS), :] = zero_row

        @pl.when(jnp.logical_not(gets_two))
        def _():
            for k in range(2):
                pads[step, (1 - vt) * (ROWS + 2) + k, pl.ds(TOP, COLS), :] = zero_row

        for side, present in sides:
            @pl.when(jnp.logical_not(present))
            def _():
                for group in range(2):
                    for part in range(2):
                        halos[step, group, side, part] = jnp.zeros((8, LOCAL), F32)

    def take_x(step):
        pl.when(gets_two)(lambda: x_wait(step, 2).wait_recv())
        pl.when(jnp.logical_not(gets_two))(lambda: x_wait(step, 1).wait_recv())

    def take_y(step, group):
        for side, present in sides:
            pl.when(present)(lambda side=side: y_copy(step, group, side, side).wait_recv())
            y = TOP - 2 + side * (COLS + 2)
            for x in range(GROUP):
                at = 2 * (x % 4)
                pads[step, 2 + bases[group] + x, y:y + 2, :] = halos[step, group, side, x // 4, at:at + 2, :]

    def wait_sent(step):
        pl.when(gets_two)(lambda: x_copy(step, 1).wait_send())
        pl.when(jnp.logical_not(gets_two))(lambda: x_copy(step, 2).wait_send())
        for group in range(2):
            for side, present in sides:
                pl.when(present)(lambda side=side, group=group: y_copy(step, group, side, side).wait_send())

    parts = ((0, 2 * gx, GROUP - 2), (0, (1 - gx) * (GROUP - 2), 2), (1, 0, GROUP))

    def store(part):
        group, row, rows = parts[part]
        at = pl.ds(bases[group] + row, rows)
        return pltpu.make_async_copy(out.at[at], result.at[at], store_sem.at[part])

    def there(step, part):
        group, row, rows = parts[part]
        at = cell_range(row, rows)
        return pltpu.make_async_remote_copy(
            src_ref=yown.at[step, group, :, at, :], dst_ref=yin.at[step, group, :, at, :],
            send_sem=fsend.at[step, part], recv_sem=frecv.at[step, part],
            device_id=(gx, gy, 1 - vt), device_id_type=MESH)

    def back(step, group, k):
        return pltpu.make_async_remote_copy(
            src_ref=gown.at[step, group, k], dst_ref=gin.at[step, group, k],
            send_sem=qsend.at[step, group, k], recv_sem=qrecv.at[step, group, k],
            device_id=(gx, gy, 1 - vt), device_id_type=MESH)

    def stage_a(step, part):
        group, row, rows = parts[part]
        advect(vt, pads.at[step], bases[group], row, rows, adv.at[group])

    def stage_t(step, part):
        group, row, rows = parts[part]
        to_parities(vt, adv.at[group], row, rows, h_ref, t_ref, yown.at[step, group])
        there(step, part).start()

    def stage_c(step, group):
        for part in ((0, 1), (2,))[group]:
            there(step, part).wait_recv()
        contract(vt, yown.at[step, group], yin.at[step, group], khi, klo, gown.at[step, group],
                 lambda k: back(step, group, k).start())

    def stage_f(step, part):
        group, row, rows = parts[part]
        base = bases[group]
        if step < STEPS - 1:
            def put(lanes, value):
                pads[step + 1, pl.ds(2 + base + row, rows), TOP:TOP + COLS, lanes] = value
        else:
            def put(lanes, value):
                out[pl.ds(base + row, rows), :, lanes] = value
        cells = pl.ds(pl.multiple_of(base * COLS, CELLS), CELLS)
        from_parities(vt, gown.at[step, group], gin.at[step, group], row, rows, h_ref, t_ref, adv.at[group],
                      dens_b.at[cells], type_b.at[cells], inflow, put)

        if step == STEPS - 1:
            store(part).start()

    def take_gains(step, group):
        for k in range(2):
            back(step, group, k).wait_recv()

    load.wait()
    pl.semaphore_wait(barrier, 2 + has_left.astype(jnp.int32) + has_right.astype(jnp.int32))
    send_x(0)
    for group in range(2):
        send_y(0, group)
    for step in range(STEPS):
        clear_missing(step)
    for copy in small:
        copy.wait()
    rate = (COLLISION_RATE * density[...]).T
    kind = as_f32(cell_type[...]).T
    for x in range(ROWS):
        dens_b[x * COLS:x * COLS + COLS] = jnp.broadcast_to(rate[:, x:x + 1], (COLS, 128))
        type_b[x * COLS:x * COLS + COLS] = jnp.broadcast_to(kind[:, x:x + 1], (COLS, 128))
    parity_maps(vt, h_ref)
    make_kernel_blocks(vt, khi, klo)

    for step in range(STEPS):
        final = step == STEPS - 1
        take_y(step, 1)
        stage_a(step, 2)
        stage_t(step, 2)
        take_y(step, 0)
        stage_a(step, 0)
        stage_t(step, 0)
        stage_c(step, 1)
        take_x(step)
        stage_a(step, 1)
        stage_t(step, 1)
        take_gains(step, 1)
        stage_f(step, 2)
        if not final:
            send_y(step + 1, 1)
        stage_c(step, 0)
        take_gains(step, 0)
        stage_f(step, 1)
        if not final:
            send_x(step + 1)
        stage_f(step, 0)
        if not final:
            send_y(step + 1, 0)
    for part in range(3):
        store(part).wait()
    for step in range(STEPS):
        wait_sent(step)
        for part in range(3):
            there(step, part).wait_send()
        for group in range(2):
            for k in range(2):
                back(step, group, k).wait_send()


def per_device(distribution, density, cell_type, inflow):
    dma = pltpu.SemaphoreType.DMA
    pair = pltpu.VMEM((STEPS, 2, 2, CELLS, 1024), F32)
    return pl.pallas_call(
        kernel,
        out_shape=jax.ShapeDtypeStruct((ROWS, COLS, LOCAL), F32),
        in_specs=[pl.BlockSpec(memory_space=pltpu.HBM)] * 4,
        out_specs=pl.BlockSpec(memory_space=pl.ANY),
        scratch_shapes=[
            pltpu.VMEM((STEPS, PAD_X, PAD_Y, LOCAL), F32),
            pltpu.VMEM((STEPS, 2, 2, 2, 8, LOCAL), F32),
            pltpu.VMEM((STEPS, 2, 2, 2, 8, LOCAL), F32),
            pltpu.VMEM((2, GROUP, COLS, LOCAL), F32),
            pair, pair, pair, pair,
            pltpu.VMEM((2048, 256), BF16),
            pltpu.VMEM((2, 1024, 1024), BF16),
            pltpu.VMEM((2, 1024, 1024), BF16),
            pltpu.VMEM((2, 256, 256), BF16),
            pltpu.VMEM((ROWS * COLS, 128), F32),
            pltpu.VMEM((ROWS * COLS, 128), F32),
            pltpu.VMEM((ROWS, COLS, LOCAL), F32),
            pltpu.VMEM((ROWS, COLS), F32),
            pltpu.VMEM((ROWS, COLS), jnp.int32),
            pltpu.VMEM((1, LOCAL), F32),
            dma((4,)), dma((3,)),
            dma((STEPS,)), dma((STEPS,)),
            dma((STEPS, 2, 2)), dma((STEPS, 2, 2)),
            dma((STEPS, 3)), dma((STEPS, 3)),
            dma((STEPS, 2, 2)), dma((STEPS, 2, 2)),
        ],
        compiler_params=pltpu.CompilerParams(
            collective_id=0, has_side_effects=True, vmem_limit_bytes=46 << 20),
    )(*(pltpu.with_memory_space_constraint(x, pltpu.HBM)
        for x in (distribution, density, cell_type, inflow.reshape(1, LOCAL))))


def solution(mesh):
    placed = (P("gx", "gy", "vert"), P("gx", "gy"), P("gx", "gy"), P("vert"))
    return jax.shard_map(
        per_device, mesh=mesh, in_specs=placed, out_specs=P("gx", "gy", "vert"), check_vma=False
    )
```
